1024 devices in a mesh: ctx: 64 (over x, y_hi, core), fsdp: 8 (over z), batch: 2 (over y_lo).
Axes of the slice: x: 8, y: 8 (y_hi: 4, y_lo: 2; y = y_hi * 2 + y_lo), z: 8, core: 2. Of those that a mesh axis runs over, the one named last changes fastest.
Arguments:
- inputs: bfloat16 [2, 8192, 4096], P('batch', 'ctx'), may hold values from -6 to 6
- values: bfloat16 [2, 8192, 2048], P('batch', 'ctx', 'fsdp'), may hold values from -6 to 6
- w_qk: bfloat16 [4096, 256], P('fsdp'), may hold values from -0.09375 to 0.09375
- conv_qk: float32 [3, 256], P(None, 'fsdp'), may hold values from -3 to 3
- conv_v: float32 [3, 2048], P(None, 'fsdp'), may hold values from -3 to 3
- d_attn: bfloat16 [2, 8192, 2048], P('batch', 'ctx', 'fsdp'), may hold values from -6 to 6
Outputs:
- attended: bfloat16 [2, 8192, 2048], P('batch', 'ctx', 'fsdp')
- grad_v: bfloat16 [2, 8192, 2048], P('batch', 'ctx', 'fsdp')
- grad_w: float32 [4096, 256], P(('ctx', 'batch'), 'fsdp')
The draws below stay inside these ranges and needn't reach their ends.
All inputs are finite; a program needn't handle non-finite values.
Results may differ from the reference program's by a relative error of at most 0.013.
Values may be sent and summed in bfloat16 or wider, within the bound.
No kernel may reach another device: no remote copies, remote signals or barrier semaphores. Data moves between devices by JAX's collectives and lax.ppermute only.
A program may use at most 32 MiB of HBM per device.

```python
import jax
import jax.numpy as jnp
from jax import lax

D = 4096
H = 8
F = 16
E = 256
CONV = 3
TOK_DEV = 128
QK = 256
V = 2048
SEQS = 2
LENGTH = 8192
N_CTX = 64


def steps_of(own_key, extent, split, smallest, high):
    gain = 1.0
    for position, blocks in split:
        heights = jax.random.uniform(jax.random.fold_in(jax.random.fold_in(own_key, 6), position), (blocks,), jnp.float32, smallest / len(split), high / len(split))
        gain = gain * jnp.repeat(jnp.exp(heights), extent[position] // blocks).reshape((-1,) + (1,) * (len(extent) - 1 - position))
    return gain


def centred(rng, shape, scale, reach, split=(), dtype=jnp.bfloat16):
    level = steps_of(rng, shape, split, -0.22, 0.18) if split else 1.0
    result = jax.random.normal(rng, shape, jnp.float32) * scale * level
    return jnp.minimum(jnp.maximum(result, -reach), reach).astype(dtype)


def setup_inputs(seed: int = 0) -> dict:
    streams_of = jax.random.split(jax.random.key(seed), 7)
    return {
        "inputs": centred(streams_of[0], (SEQS, LENGTH, D), 1.0, 6.0, ((0, 2), (1, 64))),
        "values": centred(streams_of[1], (SEQS, LENGTH, V), 1.0, 6.0, ((0, 2), (1, 64), (2, 8))),
        "w_qk": centred(streams_of[2], (D, QK), D ** -0.5, 0.09375, ((0, 8),)),
        "conv_qk": centred(streams_of[3], (CONV, QK), 0.6, 3.0, ((1, 8),), jnp.float32),
        "conv_v": centred(streams_of[4], (CONV, V), 0.6, 3.0, ((1, 8),), jnp.float32),
        "d_attn": centred(streams_of[5], (SEQS, LENGTH, V), 1.0, 6.0, ((0, 2), (1, 64), (2, 8))),
    }


eps_norm = 1e-05
highest = lax.Precision.HIGHEST

def rounded(array):
    return lax.optimization_barrier(array.astype(jnp.bfloat16)).astype(jnp.float32)

def features(vector):
    leading = vector.shape[:-1]
    quadratic = (vector[..., :, None] * vector[..., None, :]).reshape(leading + (F * F,))
    constant = jnp.ones(leading + (1,), jnp.float32)
    return jnp.concatenate([constant, vector * F ** (-0.25), quadratic * (2.0 * F) ** (-0.5)], axis=-1)

def features_back(vector, upstream):
    leading = vector.shape[:-1]
    linear = upstream[..., 1:1 + F]
    square = upstream[..., 1 + F:].reshape(leading + (F, F))
    paired = lax.optimization_barrier(jnp.sum(square * vector[..., None, :], axis=-1)) + lax.optimization_barrier(jnp.sum(square * vector[..., :, None], axis=-2))
    return linear * F ** (-0.25) + paired * (2.0 * F) ** (-0.5)

def split_heads(block):
    paired = block[..., :QK].reshape(block.shape[:-1] + (H, 2 * F)).astype(jnp.float32)
    queries = paired[..., :F]
    key_rows = paired[..., F:]
    valued = block[..., QK:].reshape(block.shape[:-1] + (H, E)).astype(jnp.float32)
    return (queries, key_rows, valued)

def block_kernel(queries, key_rows):
    dotted = jnp.einsum('sthf,sphf->shtp', queries, key_rows) * F ** (-0.5)
    rows_at = lax.broadcasted_iota(jnp.int32, (TOK_DEV, TOK_DEV), 0)
    cols_at = lax.broadcasted_iota(jnp.int32, (TOK_DEV, TOK_DEV), 1)
    causal = (cols_at <= rows_at)[None, None]
    kernel = jnp.where(causal, 1.0 + dotted + 0.5 * dotted * dotted, 0.0)
    return (dotted, causal, kernel)

def to_blocks(array):
    return array.reshape(SEQS, N_CTX, TOK_DEV, array.shape[-1]).transpose(1, 0, 2, 3)

def from_blocks(array):
    return array.transpose(1, 0, 2, 3).reshape(SEQS, LENGTH, array.shape[-1])

def local_state(block):
    queries, key_rows, valued = split_heads(block)
    return jnp.einsum('sphf,sphe->sfhe', features(key_rows), valued, precision=highest)

def forward_block(operands):
    block, prior, upstream = operands
    queries, key_rows, valued = split_heads(block)
    dotted, causal, kernel = block_kernel(queries, key_rows)
    kernel_b = rounded(kernel)
    mixed_out = jnp.einsum('shtp,sphe->sthe', kernel_b, valued)
    mixed_out = mixed_out + jnp.einsum('sthf,sfhe->sthe', features(queries), prior, precision=highest)
    scale_inv = lax.rsqrt(lax.optimization_barrier(jnp.mean(mixed_out * mixed_out, axis=-1, keepdims=True)) + eps_norm)
    normed = mixed_out * scale_inv
    attended = normed.astype(jnp.bfloat16).reshape(SEQS, TOK_DEV, V)
    grad_in = upstream.astype(jnp.float32).reshape(SEQS, TOK_DEV, H, E)
    d_mixed = (scale_inv * (grad_in - normed * lax.optimization_barrier(jnp.mean(grad_in * normed, axis=-1, keepdims=True)))).astype(jnp.bfloat16)
    d_state = jnp.einsum('sthf,sthe->sfhe', features(queries), d_mixed.astype(jnp.float32), precision=highest)
    return (attended, d_mixed, d_state)

def backward_block(operands):
    block, prior, later, d_mixed = operands
    queries, key_rows, valued = split_heads(block)
    dotted, causal, kernel = block_kernel(queries, key_rows)
    kernel_b = rounded(kernel)
    d_mixed32 = d_mixed.astype(jnp.float32)
    d_kernel = jnp.einsum('sthe,sphe->shtp', d_mixed32, valued)
    d_score = rounded(jnp.where(causal, d_kernel * (1.0 + dotted), 0.0) * F ** (-0.5))
    d_query = jnp.einsum('shtp,sphf->sthf', d_score, key_rows)
    d_query = d_query + features_back(queries, jnp.einsum('sthe,sfhe->sthf', d_mixed32, prior, precision=highest))
    d_key = jnp.einsum('shtp,sthf->sphf', d_score, queries)
    d_key = d_key + features_back(key_rows, jnp.einsum('sphe,sfhe->sphf', valued, later, precision=highest))
    d_valued = jnp.einsum('shtp,sthe->sphe', kernel_b, d_mixed32)
    d_valued = d_valued + jnp.einsum('sphf,sfhe->sphe', features(key_rows), later, precision=highest)
    d_paired = jnp.concatenate([d_query, d_key], axis=-1).reshape(SEQS, TOK_DEV, QK)
    return jnp.concatenate([d_paired, d_valued.reshape(SEQS, TOK_DEV, V)], axis=-1)

def reference(inputs, values, w_qk, conv_qk, conv_v, d_attn):
    conv_w = jnp.concatenate([conv_qk, conv_v], axis=1)
    qk_raw = jnp.dot(inputs.reshape(SEQS * LENGTH, D), w_qk, preferred_element_type=jnp.float32)
    qk_raw = qk_raw.astype(jnp.bfloat16).reshape(SEQS, LENGTH, QK)
    joined = jnp.concatenate([qk_raw, values], axis=-1)
    running = jnp.zeros(joined.shape, jnp.float32)
    for offset in range(CONV):
        moved = jnp.pad(joined, ((0, 0), (offset, 0), (0, 0)))[:, :LENGTH, :]
        running = running + conv_w[offset] * moved.astype(jnp.float32)
    convolved = to_blocks(running.astype(jnp.bfloat16))
    upstream = to_blocks(d_attn)
    states = lax.map(local_state, convolved)
    zero_state = jnp.zeros((1,) + states.shape[1:], jnp.float32)
    prefix = jnp.concatenate([zero_state, jnp.cumsum(states, axis=0)[:-1]], axis=0)
    attended, d_mixed, d_states = lax.map(forward_block, (convolved, prefix, upstream))
    from_end = jnp.flip(jnp.cumsum(jnp.flip(d_states, axis=0), axis=0), axis=0)
    suffix = jnp.concatenate([from_end[1:], zero_state], axis=0)
    d_joined = from_blocks(lax.map(backward_block, (convolved, prefix, suffix, d_mixed)))
    running = jnp.zeros(d_joined.shape, jnp.float32)
    for offset in range(CONV):
        moved = jnp.pad(d_joined, ((0, 0), (0, offset), (0, 0)))[:, offset:, :]
        running = running + conv_w[offset] * moved
    grad_v = running[..., QK:].astype(jnp.bfloat16)
    d_qk = running[..., :QK].astype(jnp.bfloat16)
    grad_w = lax.dot_general(inputs.reshape(SEQS * LENGTH, D), d_qk.reshape(SEQS * LENGTH, QK), (((0,), (0,)), ((), ())), preferred_element_type=jnp.float32)
    grad_w = grad_w * (SEQS * LENGTH) ** (-0.5)
    attended = from_blocks(attended)
    return (attended, grad_v, grad_w)
```

```python
import jax
import jax.numpy as jnp
from jax import lax
from jax.experimental import pallas as pl
from jax.experimental.pallas import tpu as pltpu
from jax.sharding import Mesh
from jax.sharding import PartitionSpec as P

F = 16
E = 256
CONV = 3
POS = 128
ROWS = 160
TILES = ROWS // 8 * (E // 128)
CTX = ("ctx_0", "ctx_1", "ctx_2")
CTX_BATCH = ("ctx_0", "ctx_1", "ctx_2", "batch")
BF = jnp.bfloat16
F32 = jnp.float32
eps_norm = 1e-05


def nn(a, b):
    return lax.dot_general(a, b, (((1,), (0,)), ((), ())), preferred_element_type=F32)


def nt(a, b):
    return lax.dot_general(a, b, (((1,), (1,)), ((), ())), preferred_element_type=F32)


def call(body, outs, *args, flops=0, name=None):
    moved = sum(a.size * a.dtype.itemsize for a in (*args, *outs))
    return pl.pallas_call(
        body,
        out_shape=outs,
        in_specs=[pl.BlockSpec(memory_space=pltpu.VMEM)] * len(args),
        out_specs=[pl.BlockSpec(memory_space=pltpu.VMEM)] * len(outs),
        cost_estimate=pl.CostEstimate(flops=flops, bytes_accessed=moved, transcendentals=0),
        compiler_params=pltpu.CompilerParams(vmem_limit_bytes=16 << 20),
        name=name,
    )(*args)


def struct(shape, dtype):
    return jax.ShapeDtypeStruct(shape, dtype)


def shifted(w, s):
    return w if s % F == 0 else jnp.concatenate([w[s % F :], w[: s % F]], axis=0)


def rows_of(w):
    parts = [w]
    for s in range(8):
        parts.append(w * shifted(w, s))
    parts.append(w[:8] * w[8:])
    at = lax.broadcasted_iota(jnp.int32, (8, w.shape[1]), 0)
    parts.append(jnp.where(at == 0, 1.0, 0.0).astype(F32))
    return jnp.concatenate(parts, axis=0)


def gains(rows, width):
    at = lax.broadcasted_iota(jnp.int32, (rows, width), 0)
    quad = jnp.where(at < 2 * F, 1.0 / 32.0, 1.0 / 16.0)
    return jnp.where(at < F, 0.25, jnp.where(at < 152, quad, 1.0)).astype(F32)


def rows_back(w, y):
    total = 0.25 * y[:F] + (1.0 / 16.0) * w * y[F : 2 * F]
    for s in range(1, 8):
        y_s = y[F * (s + 1) : F * (s + 2)]
        total = total + (1.0 / 16.0) * (
            shifted(w, s) * y_s + shifted(w, F - s) * shifted(y_s, F - s)
        )
    y_8 = y[144:152]
    half = jnp.concatenate([w[8:] * y_8, w[:8] * y_8], axis=0)
    return total + (1.0 / 16.0) * half


def to_tiles(state, tiles_ref):
    for tile in range(TILES):
        r, c = divmod(tile, 2)
        tiles_ref[tile] = state[8 * r : 8 * r + 8, 128 * c : 128 * c + 128].astype(BF)
    count = tiles_ref.shape[0]
    for tile in range(TILES, count):
        tiles_ref[tile] = jnp.zeros((8, 128), BF)


def from_tiles(tiles_ref):
    halves = [
        jnp.concatenate([tiles_ref[2 * r + c].astype(F32) for r in range(ROWS // 8)], axis=0)
        for c in range(2)
    ]
    return jnp.concatenate(halves, axis=1)


def turn_body(w_ref, out_ref):
    width = w_ref.shape[1]
    row = lax.broadcasted_iota(jnp.int32, (width, width), 0)
    col = lax.broadcasted_iota(jnp.int32, (width, width), 1)
    eye = jnp.where(row == col, 1.0, 0.0).astype(BF)
    turned = nt(eye, w_ref[...]).astype(BF)
    for part in range(out_ref.shape[0]):
        out_ref[part] = turned[32 * part : 32 * part + 32]


def state_body(w_ref, tok_ref, htok_ref, val_ref, hval_ref, cqk_ref, cv_ref, conv_ref, valued_ref, tiles_ref):
    parts, _, deep = w_ref.shape
    own = jnp.zeros((2 * F, POS), F32)
    rim = jnp.zeros((2 * F, htok_ref.shape[0]), F32)
    for part in range(parts):
        w = w_ref[part]
        own = own + nt(w, tok_ref[:, deep * part : deep * part + deep])
        rim = rim + nt(w, htok_ref[:, deep * part : deep * part + deep])
    x0 = own.astype(BF).astype(F32)
    h = rim.astype(BF).astype(F32)
    lane = lax.broadcasted_iota(jnp.int32, x0.shape, 1)
    last, before = (jnp.broadcast_to(h[:, k : k + 1], x0.shape) for k in (7, 6))
    x1 = jnp.where(lane == 0, last, pltpu.roll(x0, 1, 1))
    x2 = jnp.where(lane == 0, before, jnp.where(lane == 1, last, pltpu.roll(x0, 2, 1)))
    conv = cqk_ref[0] * x0 + cqk_ref[1] * x1 + cqk_ref[2] * x2
    conv = conv.astype(BF).astype(F32)
    conv_ref[...] = conv
    v0 = val_ref[...].astype(F32)
    hv = hval_ref[...].astype(F32)
    at = lax.broadcasted_iota(jnp.int32, v0.shape, 0)
    last, before = (jnp.broadcast_to(hv[k : k + 1], v0.shape) for k in (7, 6))
    v1 = jnp.where(at == 0, last, pltpu.roll(v0, 1, 0))
    v2 = jnp.where(at == 0, before, jnp.where(at == 1, last, pltpu.roll(v0, 2, 0)))
    valued = (cv_ref[0:1] * v0 + cv_ref[1:2] * v1 + cv_ref[2:3] * v2).astype(BF)
    valued_ref[...] = valued
    to_tiles(nn(rows_of(conv[F:]).astype(BF), valued), tiles_ref)


def local_body(conv_ref, valued_ref, mixed_ref, kernel_ref, slope_ref, qrows_ref, krows_ref, qturn_ref):
    conv = conv_ref[...]
    queries, keys = conv[:F], conv[F:]
    dotted = nn(queries.T.astype(BF), keys.astype(BF)) * 0.25
    row = lax.broadcasted_iota(jnp.int32, dotted.shape, 0)
    col = lax.broadcasted_iota(jnp.int32, dotted.shape, 1)
    causal = col <= row
    kernel = jnp.where(causal, 1.0 + dotted + 0.5 * dotted * dotted, 0.0)
    slope_ref[...] = jnp.where(causal, (1.0 + dotted) * 0.25, 0.0)
    mixed_ref[...] = nn(kernel.astype(BF), valued_ref[...])
    kernel_ref[...] = kernel.T.astype(BF)
    q_rows, k_rows = rows_of(queries), rows_of(keys)
    gain = gains(ROWS, POS)
    qturn_ref[...] = q_rows.astype(BF)
    qrows_ref[...] = (q_rows * gain).T.astype(BF)
    krows_ref[...] = (k_rows * gain).T.astype(BF)


def before_body(in_ref, out_ref):
    count = in_ref.shape[0]
    total = jnp.zeros(in_ref.shape[1:], F32)
    for k in range(count):
        out_ref[k] = total.astype(BF)
        total = total + in_ref[k].astype(F32)


def after_body(in_ref, out_ref):
    count = in_ref.shape[0]
    total = jnp.zeros(in_ref.shape[1:], F32)
    for k in reversed(range(count)):
        out_ref[k] = total.astype(BF)
        total = total + in_ref[k].astype(F32)


def mix_body(prior_ref, mixed_ref, qrows_ref, qturn_ref, grad_ref, att_ref, dmix_ref, rows_ref, tiles_ref):
    prior = from_tiles(prior_ref).astype(BF)
    rows_ref[...] = prior
    mixed = mixed_ref[...] + nn(qrows_ref[...], prior)
    inv = lax.rsqrt(jnp.mean(mixed * mixed, axis=-1, keepdims=True) + eps_norm)
    normed = mixed * inv
    att_ref[...] = normed.astype(BF)
    grad = grad_ref[...].astype(F32)
    d_mixed = (inv * (grad - normed * jnp.mean(grad * normed, axis=-1, keepdims=True))).astype(BF)
    dmix_ref[...] = d_mixed
    to_tiles(nn(qturn_ref[...], d_mixed), tiles_ref)


def back_body(conv_ref, valued_ref, kernel_ref, slope_ref, dmix_ref, rows_ref, dqk_ref, dval_ref):
    conv = conv_ref[...]
    queries, keys = conv[:F], conv[F:]
    d_mixed = dmix_ref[...]
    d_score = (nt(d_mixed, valued_ref[...]) * slope_ref[...]).astype(BF)
    d_query = nt(keys.astype(BF), d_score) + rows_back(queries, nt(rows_ref[...], d_mixed))
    dqk_ref[:F] = d_query
    dqk_ref[F:] = nn(queries.astype(BF), d_score)
    dval_ref[...] = nn(kernel_ref[...], d_mixed)


def grad_body(later_ref, conv_ref, valued_ref, krows_ref, dqk_ref, dval_ref, tok_ref, htok_ref, cqk_ref, cv_ref, gval_ref, head_ref, out_ref):
    later = from_tiles(later_ref).astype(BF)
    keys = conv_ref[F:]
    d_key = dqk_ref[F:] + rows_back(keys, nt(later, valued_ref[...]))
    d = jnp.concatenate([dqk_ref[:F], d_key], axis=0)
    lane = lax.broadcasted_iota(jnp.int32, d.shape, 1)
    d1, d2 = cqk_ref[1] * d, cqk_ref[2] * d
    own = cqk_ref[0] * d
    own = own + jnp.where(lane < POS - 1, pltpu.roll(d1, POS - 1, 1), 0.0)
    own = own + jnp.where(lane < POS - 2, pltpu.roll(d2, POS - 2, 1), 0.0)
    to_last = pltpu.roll(d2, 6, 1)
    rim = jnp.where(lane == 6, to_last, jnp.where(lane == 7, pltpu.roll(d1, 7, 1) + to_last, 0.0))
    own_b, rim_b = own.astype(BF), rim[:, :8].astype(BF)

    dv = dval_ref[...] + nn(krows_ref[...], later)
    head_ref[...] = dv[:8]
    at = lax.broadcasted_iota(jnp.int32, dv.shape, 0)
    gval = cv_ref[0:1] * dv
    gval = gval + cv_ref[1:2] * jnp.where(at < POS - 1, pltpu.roll(dv, POS - 1, 0), 0.0)
    gval = gval + cv_ref[2:3] * jnp.where(at < POS - 2, pltpu.roll(dv, POS - 2, 0), 0.0)
    gval_ref[...] = gval

    group = lax.broadcasted_iota(jnp.int32, (8, 128), 1) // 32
    chunk = 512
    for start in range(0, tok_ref.shape[1], chunk):
        part = nn(own_b, tok_ref[:, start : start + chunk]) + nn(rim_b, htok_ref[:, start : start + chunk])
        for at_lane in range(0, chunk, 128):
            blocks = [part[8 * i : 8 * i + 8, at_lane : at_lane + 128] for i in range(4)]
            for q in range(4):
                moved = [pltpu.roll(b, 32 * ((i - q) % 4), 1) if i != q else b for i, b in enumerate(blocks)]
                packed = jnp.where(
                    group == 0, moved[0], jnp.where(group == 1, moved[1], jnp.where(group == 2, moved[2], moved[3]))
                )
                out_ref[(start + at_lane) // 32 + q] = packed.astype(out_ref.dtype)


def rim_body(gval_ref, next_ref, cv_ref, out_ref):
    out_ref[...] = gval_ref[...].astype(BF)
    nxt = next_ref[...]
    at = lax.broadcasted_iota(jnp.int32, nxt.shape, 0)
    c1, c2 = cv_ref[1:2], cv_ref[2:3]
    first, second = (jnp.broadcast_to(nxt[k : k + 1], nxt.shape) for k in (0, 1))
    more = jnp.where(at == 6, c2 * first, jnp.where(at == 7, c1 * first + c2 * second, 0.0))
    out_ref[POS - 8 :] = (gval_ref[POS - 8 :] + more).astype(BF)


def sum_body(parts_ref, out_ref, *, scale):
    totals = [parts_ref[k].astype(F32) for k in range(8)]
    for k in range(8, parts_ref.shape[0]):
        totals[k % 8] = totals[k % 8] + parts_ref[k].astype(F32)
    while len(totals) > 1:
        totals = [a + b for a, b in zip(totals[::2], totals[1::2])]
    total = totals[0] * scale
    stacked = jnp.concatenate([total] + [pltpu.roll(total, 128 - 32 * i, 1) for i in (1, 2, 3)], axis=0)
    square = jnp.concatenate([stacked, jnp.zeros((96, 128), F32)], axis=0).T
    out_ref[...] = square[:32, :32]


def to_next(value, by):
    size = lax.axis_size(CTX)
    pairs = [(i, i + by) for i in range(size) if 0 <= i + by < size]
    return lax.ppermute(value, CTX, pairs)


def exchange(value, axes):
    return lax.all_to_all(value, axes, split_axis=0, concat_axis=0, tiled=True)


def shards(inputs, values, w_qk, conv_qk, conv_v, d_attn):
    tokens, own_values = inputs[0], values[0]
    depth = tokens.shape[1]
    splits = lax.axis_size("fsdp")
    blocks = lax.axis_size(CTX)
    peers = blocks * lax.axis_size("batch")
    deep = w_qk.shape[0]

    (turned,) = call(turn_body, [struct((splits, 2 * F, deep), BF)], w_qk, name="turn")
    weights = exchange(turned, "fsdp")
    rim = to_next(jnp.concatenate([tokens[POS - 8 :], own_values[POS - 8 :]], axis=1), 1)
    rim_tokens, rim_values = rim[:, :depth], rim[:, depth:]
    taps = jnp.broadcast_to(conv_qk[:, :, None], (CONV, 2 * F, POS))

    conv, valued, state = call(
        state_body,
        [struct((2 * F, POS), F32), struct((POS, E), BF), struct((blocks, 8, 128), BF)],
        weights, tokens, rim_tokens, own_values, rim_values, taps, conv_v,
        name="state",
    )
    states = exchange(state, CTX)
    mixed_own, kernel, slope, q_rows, k_rows, q_turn = call(
        local_body,
        [
            struct((POS, E), F32), struct((POS, POS), BF), struct((POS, POS), F32),
            struct((POS, ROWS), BF), struct((POS, ROWS), BF), struct((ROWS, POS), BF),
        ],
        conv, valued,
        flops=2 * POS * POS * (E + F), name="local",
    )
    (sums,) = call(before_body, [struct(states.shape, BF)], states, name="before")
    prior = exchange(sums, CTX)
    attended, d_mixed, prior_rows, grad_state = call(
        mix_body,
        [struct((POS, E), BF), struct((POS, E), BF), struct((ROWS, E), BF), struct((blocks, 8, 128), BF)],
        prior, mixed_own, q_rows, q_turn, d_attn[0],
        name="mix",
    )
    grad_states = exchange(grad_state, CTX)
    d_qk, d_val = call(
        back_body,
        [struct((2 * F, POS), F32), struct((POS, E), F32)],
        conv, valued, kernel, slope, d_mixed, prior_rows,
        flops=2 * POS * POS * (2 * E + 2 * F), name="back",
    )
    (grad_sums,) = call(after_body, [struct(grad_states.shape, BF)], grad_states, name="after")
    later = exchange(grad_sums, CTX)
    g_val, head, grad_parts = call(
        grad_body,
        [struct((POS, E), F32), struct((8, E), F32), struct((peers, 8, 128), BF)],
        later, conv, valued, k_rows, d_qk, d_val, tokens, rim_tokens, taps, conv_v,
        flops=2 * POS * depth * 2 * F, name="grad",
    )
    next_rows = to_next(head, -1)
    arrived = exchange(grad_parts, CTX_BATCH)
    (grad_v,) = call(rim_body, [struct((POS, E), BF)], g_val, next_rows, conv_v, name="rim")
    scale = float(POS * peers) ** (-0.5)
    (grad_w,) = call(
        lambda a, b: sum_body(a, b, scale=scale), [struct((2 * F, 2 * F), F32)], arrived, name="sum"
    )
    return (attended[None], grad_v[None], grad_w)


def solution(mesh):
    split = Mesh(
        mesh.devices.reshape(8, 4, 2, mesh.shape["fsdp"], mesh.shape["batch"]),
        ("ctx_0", "ctx_1", "ctx_2", "fsdp", "batch"),
    )
    in_specs = (
        P("batch", CTX, None),
        P("batch", CTX, "fsdp"),
        P("fsdp", None),
        P(None, "fsdp"),
        P(None, "fsdp"),
        P("batch", CTX, "fsdp"),
    )
    out_specs = (P("batch", CTX, "fsdp"), P("batch", CTX, "fsdp"), P(CTX_BATCH, "fsdp"))
    return jax.shard_map(
        shards, mesh=split, in_specs=in_specs, out_specs=out_specs, check_vma=False
    )
```

```python
import jax
import jax.numpy as jnp
from jax import lax
from jax.experimental import pallas as pl
from jax.experimental.pallas import tpu as pltpu
from jax.sharding import Mesh
from jax.sharding import PartitionSpec as P

F = 16
E = 256
CONV = 3
POS = 128
ROWS = 160
SLAB = ("ctx_1", "ctx_2")
CTX = ("ctx_0", "ctx_1", "ctx_2")
CTX_BATCH = ("ctx_0", "ctx_1", "ctx_2", "batch")
BF = jnp.bfloat16
F32 = jnp.float32
eps_norm = 1e-05


def nn(a, b):
    return lax.dot_general(a, b, (((1,), (0,)), ((), ())), preferred_element_type=F32)


def nt(a, b):
    return lax.dot_general(a, b, (((1,), (1,)), ((), ())), preferred_element_type=F32)


def tn(a, b):
    return lax.dot_general(a, b, (((0,), (0,)), ((), ())), preferred_element_type=F32)


def call(body, outs, *args, flops=0, name=None):
    moved = sum(a.size * a.dtype.itemsize for a in (*args, *outs))
    return pl.pallas_call(
        body,
        out_shape=outs,
        in_specs=[
            pl.BlockSpec(memory_space=pltpu.SMEM if a.dtype == jnp.int32 else pltpu.VMEM) for a in args
        ],
        out_specs=[pl.BlockSpec(memory_space=pltpu.VMEM)] * len(outs),
        cost_estimate=pl.CostEstimate(flops=flops, bytes_accessed=moved, transcendentals=0),
        compiler_params=pltpu.CompilerParams(vmem_limit_bytes=16 << 20),
        name=name,
    )(*args)


def struct(shape, dtype):
    return jax.ShapeDtypeStruct(shape, dtype)


def shifted(w, s):
    return w if s % F == 0 else jnp.concatenate([w[s % F :], w[: s % F]], axis=0)


def rows_of(w):
    parts = [w]
    for s in range(8):
        parts.append(w * shifted(w, s))
    parts.append(w[:8] * w[8:])
    at = lax.broadcasted_iota(jnp.int32, (8, w.shape[1]), 0)
    parts.append(jnp.where(at == 0, 1.0, 0.0).astype(F32))
    return jnp.concatenate(parts, axis=0)


def gains():
    at = lax.broadcasted_iota(jnp.int32, (1, ROWS), 1)
    quad = jnp.where(at < 2 * F, 1.0 / 32.0, 1.0 / 16.0)
    return jnp.where(at < F, 0.25, jnp.where(at < 152, quad, 1.0)).astype(F32)


def eye(size):
    row = lax.broadcasted_iota(jnp.int32, (size, size), 0)
    col = lax.broadcasted_iota(jnp.int32, (size, size), 1)
    return jnp.where(row == col, 1.0, 0.0).astype(BF)


def rows_back(w, y):
    total = 0.25 * y[:F] + (1.0 / 16.0) * w * y[F : 2 * F]
    for s in range(1, 8):
        y_s = y[F * (s + 1) : F * (s + 2)]
        total = total + (1.0 / 16.0) * (
            shifted(w, s) * y_s + shifted(w, F - s) * shifted(y_s, F - s)
        )
    y_8 = y[144:152]
    half = jnp.concatenate([w[8:] * y_8, w[:8] * y_8], axis=0)
    return total + (1.0 / 16.0) * half


def turn_body(w_ref, out_ref):
    turned = nt(eye(w_ref.shape[1]), w_ref[...]).astype(BF)
    for part in range(out_ref.shape[0]):
        out_ref[part] = turned[32 * part : 32 * part + 32]


def values_body(val_ref, hval_ref, grad_ref, cv_ref, out_ref):
    v0 = val_ref[...].astype(F32)
    hv = hval_ref[...].astype(F32)
    at = lax.broadcasted_iota(jnp.int32, v0.shape, 0)
    last, before = (jnp.broadcast_to(hv[k : k + 1], v0.shape) for k in (7, 6))
    v1 = jnp.where(at == 0, last, pltpu.roll(v0, 1, 0))
    v2 = jnp.where(at == 0, before, jnp.where(at == 1, last, pltpu.roll(v0, 2, 0)))
    valued = (cv_ref[0:1] * v0 + cv_ref[1:2] * v1 + cv_ref[2:3] * v2).astype(BF)
    square = eye(E)
    out_ref[0] = nt(square, valued).astype(BF)
    out_ref[1] = nt(square, grad_ref[...]).astype(BF)


def spread_body(w_ref, tok_ref, htok_ref, turned_ref, cqk_ref, out_ref):
    parts, _, deep = w_ref.shape
    own = jnp.zeros((2 * F, POS), F32)
    rim = jnp.zeros((2 * F, htok_ref.shape[0]), F32)
    for part in range(parts):
        w = w_ref[part]
        own = own + nt(w, tok_ref[:, deep * part : deep * part + deep])
        rim = rim + nt(w, htok_ref[:, deep * part : deep * part + deep])
    x0 = own.astype(BF).astype(F32)
    h = rim.astype(BF).astype(F32)
    lane = lax.broadcasted_iota(jnp.int32, x0.shape, 1)
    last, before = (jnp.broadcast_to(h[:, k : k + 1], x0.shape) for k in (7, 6))
    x1 = jnp.where(lane == 0, last, pltpu.roll(x0, 1, 1))
    x2 = jnp.where(lane == 0, before, jnp.where(lane == 1, last, pltpu.roll(x0, 2, 1)))
    conv = (cqk_ref[0] * x0 + cqk_ref[1] * x1 + cqk_ref[2] * x2).astype(BF)
    for peer in range(out_ref.shape[0]):
        out_ref[peer, :32] = turned_ref[0, 32 * peer : 32 * peer + 32]
        out_ref[peer, 32:64] = turned_ref[1, 32 * peer : 32 * peer + 32]
        out_ref[peer, 64:] = conv


def state_body(in_ref, before_ref, krows_ref, out_ref):
    blocks = in_ref.shape[0]
    total = jnp.zeros((32, ROWS), F32)
    for b in range(blocks):
        k_rows = rows_of(in_ref[b, 80:].astype(F32)).astype(BF)
        krows_ref[b] = k_rows
        before_ref[b] = total
        total = total + nt(in_ref[b, :32], k_rows)
    total = total.astype(BF)
    for peer in range(out_ref.shape[0]):
        out_ref[peer] = total


def local_body(in_ref, mixed_ref, kernel_ref, slope_ref, qrows_ref):
    row = lax.broadcasted_iota(jnp.int32, (POS, POS), 0)
    col = lax.broadcasted_iota(jnp.int32, (POS, POS), 1)
    causal = row <= col
    for b in range(in_ref.shape[0]):
        queries = in_ref[b, 64:80]
        dotted = tn(in_ref[b, 80:], queries) * 0.25
        kernel = jnp.where(causal, 1.0 + dotted + 0.5 * dotted * dotted, 0.0).astype(BF)
        slope_ref[b] = jnp.where(causal, (1.0 + dotted) * 0.25, 0.0)
        kernel_ref[b] = kernel
        mixed_ref[b] = nn(in_ref[b, :32], kernel)
        qrows_ref[b] = rows_of(queries.astype(F32)).astype(BF)


def mix_body(at_ref, sums_ref, before_ref, in_ref, local_ref, qrows_ref, mixed_ref, prior_ref, out_ref):
    at = at_ref[0]
    total = jnp.zeros((32, ROWS), F32)
    for x in range(sums_ref.shape[0]):
        total = total + jnp.where(x < at, sums_ref[x].astype(F32), 0.0)
    gain = gains()
    squares, products = [], []
    for b in range(in_ref.shape[0]):
        prior = before_ref[b] + total
        prior_ref[b] = prior.astype(BF)
        mixed = local_ref[b] + nn((prior * gain).astype(BF), qrows_ref[b])
        mixed_ref[b] = mixed
        squares.append(jnp.sum(mixed * mixed, axis=0, keepdims=True))
        products.append(jnp.sum(in_ref[b, 32:64].astype(F32) * mixed, axis=0, keepdims=True))
    rows = jnp.concatenate(squares + products, axis=0)
    for peer in range(out_ref.shape[0]):
        out_ref[peer] = rows


def norm_body(sums_ref, in_ref, mixed_ref, qrows_ref, att_ref, dmix_ref, after_ref, out_ref):
    rows = sums_ref[0]
    for peer in range(1, sums_ref.shape[0]):
        rows = rows + sums_ref[peer]
    rows = rows * (1.0 / E)
    blocks = in_ref.shape[0]
    total = jnp.zeros((32, ROWS), F32)
    for b in reversed(range(blocks)):
        inv = lax.rsqrt(rows[b : b + 1] + eps_norm)
        normed = mixed_ref[b] * inv
        att_ref[b] = normed.astype(BF)
        grad = in_ref[b, 32:64].astype(F32)
        d_mixed = (inv * (grad - normed * (inv * rows[blocks + b : blocks + b + 1]))).astype(BF)
        dmix_ref[b] = d_mixed
        after_ref[b] = total
        total = total + nt(d_mixed, qrows_ref[b])
    total = total.astype(BF)
    for peer in range(out_ref.shape[0]):
        out_ref[peer] = total


def back_body(in_ref, kernel_ref, slope_ref, dmix_ref, prior_ref, dqk_ref, dval_ref):
    for b in range(in_ref.shape[0]):
        queries, keys = in_ref[b, 64:80], in_ref[b, 80:]
        d_mixed = dmix_ref[b]
        d_score = (tn(in_ref[b, :32], d_mixed) * slope_ref[b]).astype(BF)
        dqk_ref[b, :F] = nn(keys, d_score) + rows_back(queries.astype(F32), tn(prior_ref[b], d_mixed))
        dqk_ref[b, F:] = nt(queries, d_score)
        dval_ref[b] = nt(d_mixed, kernel_ref[b])


def later_body(at_ref, sums_ref, after_ref, in_ref, krows_ref, dqk_ref, dval_ref, att_ref, out_ref):
    at = at_ref[0]
    total = jnp.zeros((32, ROWS), F32)
    for x in range(sums_ref.shape[0]):
        total = total + jnp.where(x > at, sums_ref[x].astype(F32), 0.0)
    gain = gains()
    for b in range(in_ref.shape[0]):
        later = after_ref[b] + total
        out_ref[b, :F] = dqk_ref[b, :F].astype(BF)
        keys = in_ref[b, 80:].astype(F32)
        d_key = dqk_ref[b, F:] + rows_back(keys, tn(later.astype(BF), in_ref[b, :32]))
        out_ref[b, F : 2 * F] = d_key.astype(BF)
        out_ref[b, 32:64] = att_ref[b]
        out_ref[b, 64:] = (dval_ref[b] + nn((later * gain).astype(BF), krows_ref[b])).astype(BF)


def grad_body(sums_ref, tok_ref, htok_ref, cqk_ref, out_ref):
    d = sums_ref[0, : 2 * F].astype(F32)
    for peer in range(1, sums_ref.shape[0]):
        d = d + sums_ref[peer, : 2 * F].astype(F32)
    lane = lax.broadcasted_iota(jnp.int32, d.shape, 1)
    d1, d2 = cqk_ref[1] * d, cqk_ref[2] * d
    own = cqk_ref[0] * d
    own = own + jnp.where(lane < POS - 1, pltpu.roll(d1, POS - 1, 1), 0.0)
    own = own + jnp.where(lane < POS - 2, pltpu.roll(d2, POS - 2, 1), 0.0)
    to_last = pltpu.roll(d2, 6, 1)
    rim = jnp.where(lane == 6, to_last, jnp.where(lane == 7, pltpu.roll(d1, 7, 1) + to_last, 0.0))
    own_b, rim_b = own.astype(BF), rim[:, :8].astype(BF)
    group = lax.broadcasted_iota(jnp.int32, (8, 128), 1) // 32
    chunk = 512
    for start in range(0, tok_ref.shape[1], chunk):
        part = nn(own_b, tok_ref[:, start : start + chunk]) + nn(rim_b, htok_ref[:, start : start + chunk])
        for at_lane in range(0, chunk, 128):
            blocks = [part[8 * i : 8 * i + 8, at_lane : at_lane + 128] for i in range(4)]
            for q in range(4):
                moved = [pltpu.roll(b, 32 * ((i - q) % 4), 1) if i != q else b for i, b in enumerate(blocks)]
                packed = jnp.where(
                    group == 0, moved[0], jnp.where(group == 1, moved[1], jnp.where(group == 2, moved[2], moved[3]))
                )
                out_ref[(start + at_lane) // 32 + q] = packed.astype(out_ref.dtype)


def return_body(in_ref, cv_ref, att_ref, gval_ref, head_ref):
    square = eye(POS)
    peers = range(in_ref.shape[0])
    att = jnp.concatenate([in_ref[j, 32:64] for j in peers], axis=0)
    d_rows = jnp.concatenate([in_ref[j, 64:] for j in peers], axis=0)
    att_ref[...] = nt(square, att).astype(BF)
    dv = nt(square, d_rows)
    head_ref[...] = dv[:8]
    at = lax.broadcasted_iota(jnp.int32, dv.shape, 0)
    gval = cv_ref[0:1] * dv
    gval = gval + cv_ref[1:2] * jnp.where(at < POS - 1, pltpu.roll(dv, POS - 1, 0), 0.0)
    gval = gval + cv_ref[2:3] * jnp.where(at < POS - 2, pltpu.roll(dv, POS - 2, 0), 0.0)
    gval_ref[...] = gval


def rim_body(gval_ref, next_ref, cv_ref, out_ref):
    out_ref[...] = gval_ref[...].astype(BF)
    nxt = next_ref[...]
    at = lax.broadcasted_iota(jnp.int32, nxt.shape, 0)
    c1, c2 = cv_ref[1:2], cv_ref[2:3]
    first, second = (jnp.broadcast_to(nxt[k : k + 1], nxt.shape) for k in (0, 1))
    more = jnp.where(at == 6, c2 * first, jnp.where(at == 7, c1 * first + c2 * second, 0.0))
    out_ref[POS - 8 :] = (gval_ref[POS - 8 :] + more).astype(BF)


def sum_body(parts_ref, out_ref, *, scale):
    totals = [parts_ref[k].astype(F32) for k in range(8)]
    for k in range(8, parts_ref.shape[0]):
        totals[k % 8] = totals[k % 8] + parts_ref[k].astype(F32)
    while len(totals) > 1:
        totals = [a + b for a, b in zip(totals[::2], totals[1::2])]
    total = totals[0] * scale
    stacked = jnp.concatenate([total] + [pltpu.roll(total, 128 - 32 * i, 1) for i in (1, 2, 3)], axis=0)
    square = jnp.concatenate([stacked, jnp.zeros((96, 128), F32)], axis=0).T
    out_ref[...] = square[:32, :32]


def to_next(value, axes, by):
    size = lax.axis_size(axes)
    pairs = [(i, i + by) for i in range(size) if 0 <= i + by < size]
    return lax.ppermute(value, axes, pairs)


def exchange(value, axes):
    return lax.all_to_all(value, axes, split_axis=0, concat_axis=0, tiled=True)


def shards(inputs, values, w_qk, conv_qk, conv_v, d_attn):
    tokens, own_values = inputs[0], values[0]
    depth = tokens.shape[1]
    splits = lax.axis_size("fsdp")
    lines = lax.axis_size("ctx_0")
    blocks = lax.axis_size(SLAB)
    peers = lax.axis_size(CTX_BATCH)
    deep = w_qk.shape[0]
    place = lax.axis_index("ctx_0").astype(jnp.int32).reshape(1)

    (turned,) = call(turn_body, [struct((splits, 2 * F, deep), BF)], w_qk, name="turn")
    weights = exchange(turned, "fsdp")
    rim = to_next(jnp.concatenate([tokens[POS - 8 :], own_values[POS - 8 :]], axis=1), CTX, 1)
    rim_tokens, rim_values = rim[:, :depth], rim[:, depth:]
    taps = jnp.broadcast_to(conv_qk[:, :, None], (CONV, 2 * F, POS))

    (value_rows,) = call(
        values_body, [struct((2, E, POS), BF)], own_values, rim_values, d_attn[0], conv_v, name="values"
    )
    (spread,) = call(
        spread_body, [struct((blocks, 96, POS), BF)], weights, tokens, rim_tokens, value_rows, taps, name="spread"
    )
    slab = exchange(spread, SLAB)
    before, k_rows, state = call(
        state_body,
        [struct((blocks, 32, ROWS), F32), struct((blocks, ROWS, POS), BF), struct((lines, 32, ROWS), BF)],
        slab,
        name="state",
    )
    states = exchange(state, "ctx_0")
    mixed_own, kernel, slope, q_rows = call(
        local_body,
        [
            struct((blocks, 32, POS), F32), struct((blocks, POS, POS), BF),
            struct((blocks, POS, POS), F32), struct((blocks, ROWS, POS), BF),
        ],
        slab,
        flops=2 * blocks * POS * POS * 48, name="local",
    )
    mixed, prior, norm = call(
        mix_body,
        [struct((blocks, 32, POS), F32), struct((blocks, 32, ROWS), BF), struct((blocks, 2 * blocks, POS), F32)],
        place, states, before, slab, mixed_own, q_rows,
        name="mix",
    )
    norms = exchange(norm, SLAB)
    att_rows, d_mixed, after, grad_state = call(
        norm_body,
        [
            struct((blocks, 32, POS), BF), struct((blocks, 32, POS), BF),
            struct((blocks, 32, ROWS), F32), struct((lines, 32, ROWS), BF),
        ],
        norms, slab, mixed, q_rows,
        name="norm",
    )
    grad_states = exchange(grad_state, "ctx_0")
    d_qk, d_val = call(
        back_body,
        [struct((blocks, 32, POS), F32), struct((blocks, 32, POS), F32)],
        slab, kernel, slope, d_mixed, prior,
        flops=2 * blocks * POS * POS * 128, name="back",
    )
    (parts,) = call(
        later_body,
        [struct((blocks, 96, POS), BF)],
        place, grad_states, after, slab, k_rows, d_qk, d_val, att_rows,
        name="later",
    )
    home = exchange(parts, SLAB)
    (grad_parts,) = call(
        grad_body,
        [struct((peers, 8, 128), BF)],
        home, tokens, rim_tokens, taps,
        flops=2 * POS * depth * 2 * F, name="grad",
    )
    arrived = exchange(grad_parts, CTX_BATCH)
    home, _ = lax.optimization_barrier((home, grad_parts))
    attended, g_val, head = call(
        return_body, [struct((POS, E), BF), struct((POS, E), F32), struct((8, E), F32)], home, conv_v, name="return"
    )
    next_rows = to_next(head, CTX, -1)
    (grad_v,) = call(rim_body, [struct((POS, E), BF)], g_val, next_rows, conv_v, name="rim")
    scale = float(POS * peers) ** (-0.5)
    (grad_w,) = call(
        lambda a, b: sum_body(a, b, scale=scale), [struct((2 * F, 2 * F), F32)], arrived, name="sum"
    )
    return (attended[None], grad_v[None], grad_w)


def solution(mesh):
    split = Mesh(
        mesh.devices.reshape(8, 4, 2, mesh.shape["fsdp"], mesh.shape["batch"]),
        ("ctx_0", "ctx_1", "ctx_2", "fsdp", "batch"),
    )
    in_specs = (
        P("batch", CTX, None),
        P("batch", CTX, "fsdp"),
        P("fsdp", None),
        P(None, "fsdp"),
        P(None, "fsdp"),
        P("batch", CTX, "fsdp"),
    )
    out_specs = (P("batch", CTX, "fsdp"), P("batch", CTX, "fsdp"), P(CTX_BATCH, "fsdp"))
    return jax.shard_map(
        shards, mesh=split, in_specs=in_specs, out_specs=out_specs, check_vma=False
    )
```

```python
import jax
import jax.numpy as jnp
from jax import lax
from jax.experimental import pallas as pl
from jax.experimental.pallas import tpu as pltpu
from jax.sharding import Mesh
from jax.sharding import PartitionSpec as P

F = 16
E = 256
CONV = 3
POS = 128
ROWS = 160
SLAB = ("ctx_1", "ctx_2")
CTX = ("ctx_0", "ctx_1", "ctx_2")
CTX_BATCH = ("ctx_0", "ctx_1", "ctx_2", "batch")
BF = jnp.bfloat16
F32 = jnp.float32
eps_norm = 1e-05


def nn(a, b):
    return lax.dot_general(a, b, (((1,), (0,)), ((), ())), preferred_element_type=F32)


def nt(a, b):
    return lax.dot_general(a, b, (((1,), (1,)), ((), ())), preferred_element_type=F32)


def tn(a, b):
    return lax.dot_general(a, b, (((0,), (0,)), ((), ())), preferred_element_type=F32)


def call(body, outs, *args, flops=0, name=None):
    moved = sum(a.size * a.dtype.itemsize for a in (*args, *outs))
    return pl.pallas_call(
        body,
        out_shape=outs,
        in_specs=[
            pl.BlockSpec(memory_space=pltpu.SMEM if a.dtype == jnp.int32 else pltpu.VMEM) for a in args
        ],
        out_specs=[pl.BlockSpec(memory_space=pltpu.VMEM)] * len(outs),
        cost_estimate=pl.CostEstimate(flops=flops, bytes_accessed=moved, transcendentals=0),
        compiler_params=pltpu.CompilerParams(vmem_limit_bytes=16 << 20),
        name=name,
    )(*args)


def struct(shape, dtype):
    return jax.ShapeDtypeStruct(shape, dtype)


def shifted(w, s):
    return w if s % F == 0 else jnp.concatenate([w[s % F :], w[: s % F]], axis=0)


def rows_of(w):
    parts = [w]
    for s in range(8):
        parts.append(w * shifted(w, s))
    parts.append(w[:8] * w[8:])
    at = lax.broadcasted_iota(jnp.int32, (8, w.shape[1]), 0)
    parts.append(jnp.where(at == 0, 1.0, 0.0).astype(F32))
    return jnp.concatenate(parts, axis=0)


def gains():
    at = lax.broadcasted_iota(jnp.int32, (1, ROWS), 1)
    quad = jnp.where(at < 2 * F, 1.0 / 32.0, 1.0 / 16.0)
    return jnp.where(at < F, 0.25, jnp.where(at < 152, quad, 1.0)).astype(F32)


def eye(size):
    row = lax.broadcasted_iota(jnp.int32, (size, size), 0)
    col = lax.broadcasted_iota(jnp.int32, (size, size), 1)
    return jnp.where(row == col, 1.0, 0.0).astype(BF)


def rows_back(w, y):
    total = 0.25 * y[:F] + (1.0 / 16.0) * w * y[F : 2 * F]
    for s in range(1, 8):
        y_s = y[F * (s + 1) : F * (s + 2)]
        total = total + (1.0 / 16.0) * (
            shifted(w, s) * y_s + shifted(w, F - s) * shifted(y_s, F - s)
        )
    y_8 = y[144:152]
    half = jnp.concatenate([w[8:] * y_8, w[:8] * y_8], axis=0)
    return total + (1.0 / 16.0) * half


def turn_body(w_ref, out_ref):
    turned = nt(eye(w_ref.shape[1]), w_ref[...]).astype(BF)
    for part in range(out_ref.shape[0]):
        out_ref[part] = turned[32 * part : 32 * part + 32]


def values_body(val_ref, hval_ref, grad_ref, cv_ref, cqk_ref, out_ref, taps_ref):
    width = cqk_ref.shape[1]
    row = lax.broadcasted_iota(jnp.int32, (width, width), 0)
    col = lax.broadcasted_iota(jnp.int32, (width, width), 1)
    for tap in range(CONV):
        spread = jnp.where(row == col, jnp.broadcast_to(cqk_ref[tap : tap + 1], (width, width)), 0.0)
        taps_ref[tap] = jnp.broadcast_to(jnp.sum(spread, axis=1, keepdims=True), (width, POS))
    v0 = val_ref[...].astype(F32)
    hv = hval_ref[...].astype(F32)
    at = lax.broadcasted_iota(jnp.int32, v0.shape, 0)
    last, before = (jnp.broadcast_to(hv[k : k + 1], v0.shape) for k in (7, 6))
    v1 = jnp.where(at == 0, last, pltpu.roll(v0, 1, 0))
    v2 = jnp.where(at == 0, before, jnp.where(at == 1, last, pltpu.roll(v0, 2, 0)))
    valued = (cv_ref[0:1] * v0 + cv_ref[1:2] * v1 + cv_ref[2:3] * v2).astype(BF)
    square = eye(E)
    out_ref[0] = nt(square, valued).astype(BF)
    out_ref[1] = nt(square, grad_ref[...]).astype(BF)


def spread_body(w_ref, tok_ref, htok_ref, turned_ref, cqk_ref, out_ref):
    parts, _, deep = w_ref.shape
    own = jnp.zeros((2 * F, POS), F32)
    rim = jnp.zeros((2 * F, htok_ref.shape[0]), F32)
    for part in range(parts):
        w = w_ref[part]
        own = own + nt(w, tok_ref[:, deep * part : deep * part + deep])
        rim = rim + nt(w, htok_ref[:, deep * part : deep * part + deep])
    x0 = own.astype(BF).astype(F32)
    h = rim.astype(BF).astype(F32)
    lane = lax.broadcasted_iota(jnp.int32, x0.shape, 1)
    last, before = (jnp.broadcast_to(h[:, k : k + 1], x0.shape) for k in (7, 6))
    x1 = jnp.where(lane == 0, last, pltpu.roll(x0, 1, 1))
    x2 = jnp.where(lane == 0, before, jnp.where(lane == 1, last, pltpu.roll(x0, 2, 1)))
    conv = (cqk_ref[0] * x0 + cqk_ref[1] * x1 + cqk_ref[2] * x2).astype(BF)
    for peer in range(out_ref.shape[0]):
        out_ref[peer, :32] = turned_ref[0, 32 * peer : 32 * peer + 32]
        out_ref[peer, 32:64] = turned_ref[1, 32 * peer : 32 * peer + 32]
        out_ref[peer, 64:] = conv


def pack(total):
    side = [total[8 * i : 8 * i + 8, POS:] for i in range(4)]
    return jnp.concatenate([total[:, :POS], jnp.concatenate(side, axis=1)], axis=0)


def unpack(packed):
    side = jnp.concatenate([packed[32:, 32 * i : 32 * i + 32] for i in range(4)], axis=0)
    return jnp.concatenate([packed[:32], side], axis=1)


def state_body(in_ref, before_ref, krows_ref, out_ref):
    blocks = in_ref.shape[0]
    total = jnp.zeros((32, ROWS), F32)
    for b in range(blocks):
        k_rows = rows_of(in_ref[b, 80:].astype(F32)).astype(BF)
        krows_ref[b] = k_rows
        before_ref[b] = total
        total = total + nt(in_ref[b, :32], k_rows)
    total = pack(total).astype(BF)
    for peer in range(out_ref.shape[0]):
        out_ref[peer] = total


def local_body(in_ref, mixed_ref, kernel_ref, slope_ref, qrows_ref):
    row = lax.broadcasted_iota(jnp.int32, (POS, POS), 0)
    col = lax.broadcasted_iota(jnp.int32, (POS, POS), 1)
    causal = row <= col
    for b in range(in_ref.shape[0]):
        queries = in_ref[b, 64:80]
        dotted = tn(in_ref[b, 80:], queries) * 0.25
        kernel = jnp.where(causal, 1.0 + dotted + 0.5 * dotted * dotted, 0.0).astype(BF)
        slope_ref[b] = jnp.where(causal, (1.0 + dotted) * 0.25, 0.0)
        kernel_ref[b] = kernel
        mixed_ref[b] = nn(in_ref[b, :32], kernel)
        qrows_ref[b] = rows_of(queries.astype(F32)).astype(BF)


def mix_body(at_ref, sums_ref, before_ref, in_ref, local_ref, qrows_ref, mixed_ref, prior_ref, out_ref):
    at = at_ref[0]
    total = jnp.zeros(sums_ref.shape[1:], F32)
    for x in range(sums_ref.shape[0]):
        total = total + jnp.where(x < at, sums_ref[x].astype(F32), 0.0)
    total = unpack(total)
    gain = gains()
    squares, products = [], []
    for b in range(in_ref.shape[0]):
        prior = before_ref[b] + total
        prior_ref[b] = prior.astype(BF)
        mixed = local_ref[b] + nn((prior * gain).astype(BF), qrows_ref[b])
        mixed_ref[b] = mixed
        squares.append(jnp.sum(mixed * mixed, axis=0, keepdims=True))
        products.append(jnp.sum(in_ref[b, 32:64].astype(F32) * mixed, axis=0, keepdims=True))
    rows = jnp.concatenate(squares + products, axis=0)
    for peer in range(out_ref.shape[0]):
        out_ref[peer] = rows


def norm_body(sums_ref, in_ref, mixed_ref, qrows_ref, att_ref, dmix_ref, after_ref, out_ref):
    rows = sums_ref[0]
    for peer in range(1, sums_ref.shape[0]):
        rows = rows + sums_ref[peer]
    rows = rows * (1.0 / E)
    blocks = in_ref.shape[0]
    total = jnp.zeros((32, ROWS), F32)
    for b in reversed(range(blocks)):
        inv = lax.rsqrt(rows[b : b + 1] + eps_norm)
        normed = mixed_ref[b] * inv
        att_ref[b] = normed.astype(BF)
        grad = in_ref[b, 32:64].astype(F32)
        d_mixed = (inv * (grad - normed * (inv * rows[blocks + b : blocks + b + 1]))).astype(BF)
        dmix_ref[b] = d_mixed
        after_ref[b] = total
        total = total + nt(d_mixed, qrows_ref[b])
    total = pack(total).astype(BF)
    for peer in range(out_ref.shape[0]):
        out_ref[peer] = total


def back_body(in_ref, kernel_ref, slope_ref, dmix_ref, prior_ref, dqk_ref, dval_ref):
    for b in range(in_ref.shape[0]):
        queries, keys = in_ref[b, 64:80], in_ref[b, 80:]
        d_mixed = dmix_ref[b]
        d_score = (tn(in_ref[b, :32], d_mixed) * slope_ref[b]).astype(BF)
        dqk_ref[b, :F] = nn(keys, d_score) + rows_back(queries.astype(F32), tn(prior_ref[b], d_mixed))
        dqk_ref[b, F:] = nt(queries, d_score)
        dval_ref[b] = nt(d_mixed, kernel_ref[b])


def later_body(at_ref, sums_ref, after_ref, in_ref, krows_ref, dqk_ref, dval_ref, att_ref, out_ref):
    at = at_ref[0]
    total = jnp.zeros(sums_ref.shape[1:], F32)
    for x in range(sums_ref.shape[0]):
        total = total + jnp.where(x > at, sums_ref[x].astype(F32), 0.0)
    total = unpack(total)
    gain = gains()
    for b in range(in_ref.shape[0]):
        later = after_ref[b] + total
        out_ref[b, :F] = dqk_ref[b, :F].astype(BF)
        keys = in_ref[b, 80:].astype(F32)
        d_key = dqk_ref[b, F:] + rows_back(keys, tn(later.astype(BF), in_ref[b, :32]))
        out_ref[b, F : 2 * F] = d_key.astype(BF)
        out_ref[b, 32:64] = att_ref[b]
        out_ref[b, 64:] = (dval_ref[b] + nn((later * gain).astype(BF), krows_ref[b])).astype(BF)


def grad_body(sums_ref, tok_ref, htok_ref, cqk_ref, out_ref):
    d = sums_ref[0, : 2 * F].astype(F32)
    for peer in range(1, sums_ref.shape[0]):
        d = d + sums_ref[peer, : 2 * F].astype(F32)
    lane = lax.broadcasted_iota(jnp.int32, d.shape, 1)
    d1, d2 = cqk_ref[1] * d, cqk_ref[2] * d
    own = cqk_ref[0] * d
    own = own + jnp.where(lane < POS - 1, pltpu.roll(d1, POS - 1, 1), 0.0)
    own = own + jnp.where(lane < POS - 2, pltpu.roll(d2, POS - 2, 1), 0.0)
    to_last = pltpu.roll(d2, 6, 1)
    rim = jnp.where(lane == 6, to_last, jnp.where(lane == 7, pltpu.roll(d1, 7, 1) + to_last, 0.0))
    own_b, rim_b = own.astype(BF), rim[:, :8].astype(BF)
    group = lax.broadcasted_iota(jnp.int32, (8, 128), 1) // 32
    chunk = 512
    for start in range(0, tok_ref.shape[1], chunk):
        part = nn(own_b, tok_ref[:, start : start + chunk]) + nn(rim_b, htok_ref[:, start : start + chunk])
        for at_lane in range(0, chunk, 128):
            blocks = [part[8 * i : 8 * i + 8, at_lane : at_lane + 128] for i in range(4)]
            for q in range(4):
                moved = [pltpu.roll(b, 32 * ((i - q) % 4), 1) if i != q else b for i, b in enumerate(blocks)]
                packed = jnp.where(
                    group == 0, moved[0], jnp.where(group == 1, moved[1], jnp.where(group == 2, moved[2], moved[3]))
                )
                out_ref[(start + at_lane) // 32 + q] = packed.astype(out_ref.dtype)


def return_body(in_ref, cv_ref, att_ref, gval_ref, head_ref):
    square = eye(POS)
    peers = range(in_ref.shape[0])
    att = jnp.concatenate([in_ref[j, 32:64] for j in peers], axis=0)
    d_rows = jnp.concatenate([in_ref[j, 64:] for j in peers], axis=0)
    att_ref[...] = nt(square, att).astype(BF)
    dv = nt(square, d_rows)
    head_ref[...] = dv[:8]
    at = lax.broadcasted_iota(jnp.int32, dv.shape, 0)
    gval = cv_ref[0:1] * dv
    gval = gval + cv_ref[1:2] * jnp.where(at < POS - 1, pltpu.roll(dv, POS - 1, 0), 0.0)
    gval = gval + cv_ref[2:3] * jnp.where(at < POS - 2, pltpu.roll(dv, POS - 2, 0), 0.0)
    gval_ref[...] = gval


def rim_body(gval_ref, next_ref, cv_ref, out_ref):
    out_ref[...] = gval_ref[...].astype(BF)
    nxt = next_ref[...]
    at = lax.broadcasted_iota(jnp.int32, nxt.shape, 0)
    c1, c2 = cv_ref[1:2], cv_ref[2:3]
    first, second = (jnp.broadcast_to(nxt[k : k + 1], nxt.shape) for k in (0, 1))
    more = jnp.where(at == 6, c2 * first, jnp.where(at == 7, c1 * first + c2 * second, 0.0))
    out_ref[POS - 8 :] = (gval_ref[POS - 8 :] + more).astype(BF)


def sum_body(parts_ref, out_ref, *, scale):
    totals = [parts_ref[k].astype(F32) for k in range(8)]
    for k in range(8, parts_ref.shape[0]):
        totals[k % 8] = totals[k % 8] + parts_ref[k].astype(F32)
    while len(totals) > 1:
        totals = [a + b for a, b in zip(totals[::2], totals[1::2])]
    total = totals[0] * scale
    stacked = jnp.concatenate([total] + [pltpu.roll(total, 128 - 32 * i, 1) for i in (1, 2, 3)], axis=0)
    square = jnp.concatenate([stacked, jnp.zeros((96, 128), F32)], axis=0).T
    out_ref[...] = square[:32, :32]


def to_next(value, axes, by):
    size = lax.axis_size(axes)
    pairs = [(i, i + by) for i in range(size) if 0 <= i + by < size]
    return lax.ppermute(value, axes, pairs)


def exchange(value, axes):
    return lax.all_to_all(value, axes, split_axis=0, concat_axis=0, tiled=True)


def shards(inputs, values, w_qk, conv_qk, conv_v, d_attn):
    tokens, own_values = inputs[0], values[0]
    depth = tokens.shape[1]
    splits = lax.axis_size("fsdp")
    lines = lax.axis_size("ctx_0")
    blocks = lax.axis_size(SLAB)
    peers = lax.axis_size(CTX_BATCH)
    deep = w_qk.shape[0]
    place = lax.axis_index("ctx_0").astype(jnp.int32).reshape(1)

    (turned,) = call(turn_body, [struct((splits, 2 * F, deep), BF)], w_qk, name="turn")
    weights = exchange(turned, "fsdp")
    rim = to_next(jnp.concatenate([tokens[POS - 8 :], own_values[POS - 8 :]], axis=1), CTX, 1)
    rim_tokens, rim_values = rim[:, :depth], rim[:, depth:]

    value_rows, taps = call(
        values_body,
        [struct((2, E, POS), BF), struct((CONV, 2 * F, POS), F32)],
        own_values, rim_values, d_attn[0], conv_v, conv_qk,
        name="values",
    )
    (spread,) = call(
        spread_body, [struct((blocks, 96, POS), BF)], weights, tokens, rim_tokens, value_rows, taps, name="spread"
    )
    slab = exchange(spread, SLAB)
    before, k_rows, state = call(
        state_body,
        [struct((blocks, 32, ROWS), F32), struct((blocks, ROWS, POS), BF), struct((lines, 40, POS), BF)],
        slab,
        name="state",
    )
    states = exchange(state, "ctx_0")
    mixed_own, kernel, slope, q_rows = call(
        local_body,
        [
            struct((blocks, 32, POS), F32), struct((blocks, POS, POS), BF),
            struct((blocks, POS, POS), F32), struct((blocks, ROWS, POS), BF),
        ],
        slab,
        flops=2 * blocks * POS * POS * 48, name="local",
    )
    mixed, prior, norm = call(
        mix_body,
        [struct((blocks, 32, POS), F32), struct((blocks, 32, ROWS), BF), struct((blocks, 2 * blocks, POS), F32)],
        place, states, before, slab, mixed_own, q_rows,
        name="mix",
    )
    norms = exchange(norm, SLAB)
    att_rows, d_mixed, after, grad_state = call(
        norm_body,
        [
            struct((blocks, 32, POS), BF), struct((blocks, 32, POS), BF),
            struct((blocks, 32, ROWS), F32), struct((lines, 40, POS), BF),
        ],
        norms, slab, mixed, q_rows,
        name="norm",
    )
    grad_states = exchange(grad_state, "ctx_0")
    d_qk, d_val = call(
        back_body,
        [struct((blocks, 32, POS), F32), struct((blocks, 32, POS), F32)],
        slab, kernel, slope, d_mixed, prior,
        flops=2 * blocks * POS * POS * 128, name="back",
    )
    (parts,) = call(
        later_body,
        [struct((blocks, 96, POS), BF)],
        place, grad_states, after, slab, k_rows, d_qk, d_val, att_rows,
        name="later",
    )
    home = exchange(parts, SLAB)
    (grad_parts,) = call(
        grad_body,
        [struct((peers, 8, 128), BF)],
        home, tokens, rim_tokens, taps,
        flops=2 * POS * depth * 2 * F, name="grad",
    )
    arrived = exchange(grad_parts, CTX_BATCH)
    home, _ = lax.optimization_barrier((home, grad_parts))
    attended, g_val, head = call(
        return_body, [struct((POS, E), BF), struct((POS, E), F32), struct((8, E), F32)], home, conv_v, name="return"
    )
    next_rows = to_next(head, CTX, -1)
    (grad_v,) = call(rim_body, [struct((POS, E), BF)], g_val, next_rows, conv_v, name="rim")
    scale = float(POS * peers) ** (-0.5)
    (grad_w,) = call(
        lambda a, b: sum_body(a, b, scale=scale), [struct((2 * F, 2 * F), F32)], arrived, name="sum"
    )
    return (attended[None], grad_v[None], grad_w)


def solution(mesh):
    split = Mesh(
        mesh.devices.reshape(8, 4, 2, mesh.shape["fsdp"], mesh.shape["batch"]),
        ("ctx_0", "ctx_1", "ctx_2", "fsdp", "batch"),
    )
    in_specs = (
        P("batch", CTX, None),
        P("batch", CTX, "fsdp"),
        P("fsdp", None),
        P(None, "fsdp"),
        P(None, "fsdp"),
        P("batch", CTX, "fsdp"),
    )
    out_specs = (P("batch", CTX, "fsdp"), P("batch", CTX, "fsdp"), P(CTX_BATCH, "fsdp"))
    return jax.shard_map(
        shards, mesh=split, in_specs=in_specs, out_specs=out_specs, check_vma=False
    )
```

```python
import jax
import jax.numpy as jnp
from jax import lax
from jax.experimental import pallas as pl
from jax.experimental.pallas import tpu as pltpu
from jax.sharding import Mesh
from jax.sharding import PartitionSpec as P

F = 16
E = 256
CONV = 3
POS = 128
ROWS = 160
SLAB = ("ctx_1", "ctx_2")
CTX = ("ctx_0", "ctx_1", "ctx_2")
CHIPS = ("ctx_0", "ctx_1", "batch")
CTX_BATCH = ("ctx_0", "ctx_1", "ctx_2", "batch")
BF = jnp.bfloat16
F32 = jnp.float32
eps_norm = 1e-05


def nn(a, b):
    return lax.dot_general(a, b, (((1,), (0,)), ((), ())), preferred_element_type=F32)


def nt(a, b):
    return lax.dot_general(a, b, (((1,), (1,)), ((), ())), preferred_element_type=F32)


def tn(a, b):
    return lax.dot_general(a, b, (((0,), (0,)), ((), ())), preferred_element_type=F32)


def call(body, outs, *args, flops=0):
    moved = sum(a.size * a.dtype.itemsize for a in (*args, *outs))
    return pl.pallas_call(
        body,
        out_shape=outs,
        in_specs=[
            pl.BlockSpec(memory_space=pltpu.SMEM if a.dtype == jnp.int32 else pltpu.VMEM) for a in args
        ],
        out_specs=[pl.BlockSpec(memory_space=pltpu.VMEM)] * len(outs),
        cost_estimate=pl.CostEstimate(flops=flops, bytes_accessed=moved, transcendentals=0),
        compiler_params=pltpu.CompilerParams(vmem_limit_bytes=8 << 20),
    )(*args)


def struct(shape, dtype):
    return jax.ShapeDtypeStruct(shape, dtype)


def shifted(w, s):
    return w if s % F == 0 else jnp.concatenate([w[s % F :], w[: s % F]], axis=0)


def rows_of(w):
    parts = [w]
    for s in range(8):
        parts.append(w * shifted(w, s))
    parts.append(w[:8] * w[8:])
    at = lax.broadcasted_iota(jnp.int32, (8, w.shape[1]), 0)
    parts.append(jnp.where(at == 0, 1.0, 0.0).astype(F32))
    return jnp.concatenate(parts, axis=0)


def gains():
    at = lax.broadcasted_iota(jnp.int32, (1, ROWS), 1)
    quad = jnp.where(at < 2 * F, 1.0 / 32.0, 1.0 / 16.0)
    return jnp.where(at < F, 0.25, jnp.where(at < 152, quad, 1.0)).astype(F32)


def eye(size):
    row = lax.broadcasted_iota(jnp.int32, (size, size), 0)
    col = lax.broadcasted_iota(jnp.int32, (size, size), 1)
    return jnp.where(row == col, 1.0, 0.0).astype(BF)


def rows_back(w, y):
    total = 0.25 * y[:F] + (1.0 / 16.0) * w * y[F : 2 * F]
    for s in range(1, 8):
        y_s = y[F * (s + 1) : F * (s + 2)]
        total = total + (1.0 / 16.0) * (
            shifted(w, s) * y_s + shifted(w, F - s) * shifted(y_s, F - s)
        )
    y_8 = y[144:152]
    half = jnp.concatenate([w[8:] * y_8, w[:8] * y_8], axis=0)
    return total + (1.0 / 16.0) * half


def turn_body(w_ref, out_ref):
    turned = nt(eye(w_ref.shape[1]), w_ref[...]).astype(BF)
    for part in range(out_ref.shape[0]):
        out_ref[part] = turned[32 * part : 32 * part + 32]


def values_body(val_ref, hval_ref, grad_ref, cv_ref, cqk_ref, out_ref, taps_ref):
    width = cqk_ref.shape[1]
    row = lax.broadcasted_iota(jnp.int32, (width, width), 0)
    col = lax.broadcasted_iota(jnp.int32, (width, width), 1)
    for tap in range(CONV):
        spread = jnp.where(row == col, jnp.broadcast_to(cqk_ref[tap : tap + 1], (width, width)), 0.0)
        taps_ref[tap] = jnp.broadcast_to(jnp.sum(spread, axis=1, keepdims=True), (width, POS))
    v0 = val_ref[...].astype(F32)
    hv = hval_ref[...].astype(F32)
    at = lax.broadcasted_iota(jnp.int32, v0.shape, 0)
    last, before = (jnp.broadcast_to(hv[k : k + 1], v0.shape) for k in (7, 6))
    v1 = jnp.where(at == 0, last, pltpu.roll(v0, 1, 0))
    v2 = jnp.where(at == 0, before, jnp.where(at == 1, last, pltpu.roll(v0, 2, 0)))
    valued = (cv_ref[0:1] * v0 + cv_ref[1:2] * v1 + cv_ref[2:3] * v2).astype(BF)
    square = eye(E)
    out_ref[0] = nt(square, valued).astype(BF)
    out_ref[1] = nt(square, grad_ref[...]).astype(BF)


def spread_body(w_ref, tok_ref, htok_ref, turned_ref, cqk_ref, out_ref):
    parts, _, deep = w_ref.shape
    own = jnp.zeros((2 * F, POS), F32)
    rim = jnp.zeros((2 * F, htok_ref.shape[0]), F32)
    for part in range(parts):
        w = w_ref[part]
        own = own + nt(w, tok_ref[:, deep * part : deep * part + deep])
        rim = rim + nt(w, htok_ref[:, deep * part : deep * part + deep])
    x0 = own.astype(BF).astype(F32)
    h = rim.astype(BF).astype(F32)
    lane = lax.broadcasted_iota(jnp.int32, x0.shape, 1)
    last, before = (jnp.broadcast_to(h[:, k : k + 1], x0.shape) for k in (7, 6))
    x1 = jnp.where(lane == 0, last, pltpu.roll(x0, 1, 1))
    x2 = jnp.where(lane == 0, before, jnp.where(lane == 1, last, pltpu.roll(x0, 2, 1)))
    conv = (cqk_ref[0] * x0 + cqk_ref[1] * x1 + cqk_ref[2] * x2).astype(BF)
    for peer in range(out_ref.shape[0]):
        out_ref[peer, :32] = turned_ref[0, 32 * peer : 32 * peer + 32]
        out_ref[peer, 32:64] = turned_ref[1, 32 * peer : 32 * peer + 32]
        out_ref[peer, 64:] = conv


def pack(total):
    side = [total[8 * i : 8 * i + 8, POS:] for i in range(4)]
    return jnp.concatenate([total[:, :POS], jnp.concatenate(side, axis=1)], axis=0)


def unpack(packed):
    side = jnp.concatenate([packed[32:, 32 * i : 32 * i + 32] for i in range(4)], axis=0)
    return jnp.concatenate([packed[:32], side], axis=1)


def state_body(in_ref, krows_ref, out_ref):
    blocks = range(in_ref.shape[0])
    for b in blocks:
        krows_ref[b] = rows_of(in_ref[b, 80:].astype(F32)).astype(BF)
    values = jnp.concatenate([in_ref[b, :32] for b in blocks], axis=1)
    total = pack(nt(values, jnp.concatenate([krows_ref[b] for b in blocks], axis=1))).astype(BF)
    for peer in range(out_ref.shape[0]):
        out_ref[peer] = total


def scores(in_ref, b):
    row = lax.broadcasted_iota(jnp.int32, (POS, POS), 0)
    col = lax.broadcasted_iota(jnp.int32, (POS, POS), 1)
    dotted = tn(in_ref[b, 80:], in_ref[b, 64:80]) * 0.25
    causal = row <= col
    return dotted, causal, jnp.where(causal, 1.0 + dotted + 0.5 * dotted * dotted, 0.0).astype(BF)


def local_body(in_ref, krows_ref, before_ref, mixed_ref, qrows_ref):
    total = jnp.zeros((32, ROWS), F32)
    for b in range(in_ref.shape[0]):
        before_ref[b] = total
        total = total + nt(in_ref[b, :32], krows_ref[b])
        mixed_ref[b] = nn(in_ref[b, :32], scores(in_ref, b)[2])
        qrows_ref[b] = rows_of(in_ref[b, 64:80].astype(F32)).astype(BF)


def mix_body(at_ref, sums_ref, before_ref, in_ref, local_ref, qrows_ref, mixed_ref, prior_ref, out_ref):
    at = at_ref[0]
    total = jnp.zeros(sums_ref.shape[1:], F32)
    for x in range(sums_ref.shape[0]):
        total = total + jnp.where(x < at, sums_ref[x].astype(F32), 0.0)
    total = unpack(total)
    gain = gains()
    squares, products = [], []
    for b in range(in_ref.shape[0]):
        prior = before_ref[b] + total
        prior_ref[b] = prior.astype(BF)
        mixed = local_ref[b] + nn((prior * gain).astype(BF), qrows_ref[b])
        mixed_ref[b] = mixed
        squares.append(jnp.sum(mixed * mixed, axis=0, keepdims=True))
        products.append(jnp.sum(in_ref[b, 32:64].astype(F32) * mixed, axis=0, keepdims=True))
    rows = jnp.concatenate(squares + products, axis=0).astype(BF)
    for peer in range(out_ref.shape[0]):
        out_ref[peer] = rows


def norm_body(sums_ref, in_ref, mixed_ref, qrows_ref, att_ref, dmix_ref, out_ref):
    rows = sums_ref[0].astype(F32)
    for peer in range(1, sums_ref.shape[0]):
        rows = rows + sums_ref[peer].astype(F32)
    rows = rows * (1.0 / E)
    blocks = in_ref.shape[0]
    for b in range(blocks):
        inv = lax.rsqrt(rows[b : b + 1] + eps_norm)
        normed = mixed_ref[b] * inv
        att_ref[b] = normed.astype(BF)
        grad = in_ref[b, 32:64].astype(F32)
        d_mixed = inv * (grad - normed * (inv * rows[blocks + b : blocks + b + 1]))
        dmix_ref[b] = d_mixed.astype(BF)
    d_all = jnp.concatenate([dmix_ref[b] for b in range(blocks)], axis=1)
    total = pack(nt(d_all, jnp.concatenate([qrows_ref[b] for b in range(blocks)], axis=1))).astype(BF)
    for peer in range(out_ref.shape[0]):
        out_ref[peer] = total


def back_body(in_ref, dmix_ref, prior_ref, qrows_ref, after_ref, dqk_ref, dval_ref):
    total = jnp.zeros((32, ROWS), F32)
    for b in reversed(range(in_ref.shape[0])):
        after_ref[b] = total
        total = total + nt(dmix_ref[b], qrows_ref[b])
        queries, keys = in_ref[b, 64:80], in_ref[b, 80:]
        d_mixed = dmix_ref[b]
        dotted, causal, kernel = scores(in_ref, b)
        slope = jnp.where(causal, (1.0 + dotted) * 0.25, 0.0)
        d_score = (tn(in_ref[b, :32], d_mixed) * slope).astype(BF)
        dqk_ref[b, :F] = nn(keys, d_score) + rows_back(queries.astype(F32), tn(prior_ref[b], d_mixed))
        dqk_ref[b, F:] = nt(queries, d_score)
        dval_ref[b] = nt(d_mixed, kernel)


def later_body(at_ref, sums_ref, after_ref, in_ref, krows_ref, dqk_ref, dval_ref, att_ref, out_ref):
    at = at_ref[0]
    total = jnp.zeros(sums_ref.shape[1:], F32)
    for x in range(sums_ref.shape[0]):
        total = total + jnp.where(x > at, sums_ref[x].astype(F32), 0.0)
    total = unpack(total)
    gain = gains()
    for b in range(in_ref.shape[0]):
        later = after_ref[b] + total
        keys = in_ref[b, 80:].astype(F32)
        d_key = dqk_ref[b, F:] + rows_back(keys, tn(later.astype(BF), in_ref[b, :32]))
        part = jnp.concatenate([dqk_ref[b, :F], d_key], axis=0).astype(BF)
        first, at_row = b - b % 2, 32 * (b % 2)
        out_ref[first, at_row : at_row + 32] = part
        out_ref[first + 1, at_row : at_row + 32] = part
        out_ref[b, 64:96] = att_ref[b]
        out_ref[b, 96:] = (dval_ref[b] + nn((later * gain).astype(BF), krows_ref[b])).astype(BF)


def grad_body(core_ref, sums_ref, tok_ref, other_ref, htok_ref, hother_ref, cqk_ref, out_ref):
    pair = sums_ref[0, : 4 * F].astype(F32)
    for peer in range(1, sums_ref.shape[0]):
        pair = pair + sums_ref[peer, : 4 * F].astype(F32)
    first, second = pair[: 2 * F], pair[2 * F :]
    core = core_ref[0]
    lane = lax.broadcasted_iota(jnp.int32, first.shape, 1)

    def ahead(d, nxt, by):
        return jnp.where(lane < POS - by, pltpu.roll(d, POS - by, 1), pltpu.roll(nxt, POS - by, 1))

    zero = jnp.zeros_like(first)
    of_first = cqk_ref[0] * first + cqk_ref[1] * ahead(first, second, 1) + cqk_ref[2] * ahead(first, second, 2)
    of_second = cqk_ref[0] * second + cqk_ref[1] * ahead(second, zero, 1) + cqk_ref[2] * ahead(second, zero, 2)
    to_last = pltpu.roll(cqk_ref[2] * first, 6, 1)
    near = pltpu.roll(cqk_ref[1] * first, 7, 1) + to_last
    rim = jnp.where(lane == 6, to_last, jnp.where(lane == 7, near, 0.0))[:, :8]
    own_b = jnp.where(core == 0, of_first, of_second).astype(BF)
    other_b = jnp.where(core == 0, of_second, of_first).astype(BF)
    rim_own = jnp.where(core == 0, rim, 0.0).astype(BF)
    rim_other = jnp.where(core == 0, 0.0, rim).astype(BF)

    group = lax.broadcasted_iota(jnp.int32, (8, 128), 1) // 32
    chunk = 512
    for start in range(0, tok_ref.shape[1], chunk):
        at = slice(start, start + chunk)
        part = nn(own_b, tok_ref[:, at]) + nn(other_b, other_ref[:, at])
        part = part + nn(rim_own, htok_ref[:, at]) + nn(rim_other, hother_ref[:, at])
        for at_lane in range(0, chunk, 128):
            cols = part[:, at_lane : at_lane + 128]
            cols = jnp.where(core == 0, cols, pltpu.roll(cols, 64, 1))
            blocks = [cols[8 * i : 8 * i + 8] for i in range(4)]
            for q in range(2):
                moved = [pltpu.roll(b, 32 * ((i - q) % 4), 1) if i != q else b for i, b in enumerate(blocks)]
                packed = jnp.where(
                    group == 0, moved[0], jnp.where(group == 1, moved[1], jnp.where(group == 2, moved[2], moved[3]))
                )
                out_ref[(start + at_lane) // 64 + q] = packed.astype(out_ref.dtype)


def return_body(in_ref, cv_ref, att_ref, gval_ref, head_ref):
    square = eye(POS)
    peers = range(in_ref.shape[0])
    att = jnp.concatenate([in_ref[j, 64:96] for j in peers], axis=0)
    d_rows = jnp.concatenate([in_ref[j, 96:] for j in peers], axis=0)
    att_ref[...] = nt(square, att).astype(BF)
    dv = nt(square, d_rows)
    head_ref[...] = dv[:8]
    at = lax.broadcasted_iota(jnp.int32, dv.shape, 0)
    gval = cv_ref[0:1] * dv
    gval = gval + cv_ref[1:2] * jnp.where(at < POS - 1, pltpu.roll(dv, POS - 1, 0), 0.0)
    gval = gval + cv_ref[2:3] * jnp.where(at < POS - 2, pltpu.roll(dv, POS - 2, 0), 0.0)
    gval_ref[...] = gval


def rim_body(gval_ref, next_ref, cv_ref, out_ref):
    out_ref[...] = gval_ref[...].astype(BF)
    nxt = next_ref[...]
    at = lax.broadcasted_iota(jnp.int32, nxt.shape, 0)
    c1, c2 = cv_ref[1:2], cv_ref[2:3]
    first, second = (jnp.broadcast_to(nxt[k : k + 1], nxt.shape) for k in (0, 1))
    more = jnp.where(at == 6, c2 * first, jnp.where(at == 7, c1 * first + c2 * second, 0.0))
    out_ref[POS - 8 :] = (gval_ref[POS - 8 :] + more).astype(BF)


def sum_body(parts_ref, out_ref, *, scale):
    totals = [parts_ref[k].astype(F32) for k in range(8)]
    for k in range(8, parts_ref.shape[0]):
        totals[k % 8] = totals[k % 8] + parts_ref[k].astype(F32)
    while len(totals) > 1:
        totals = [a + b for a, b in zip(totals[::2], totals[1::2])]
    total = totals[0] * scale
    stacked = jnp.concatenate([total] + [pltpu.roll(total, 128 - 32 * i, 1) for i in (1, 2, 3)], axis=0)
    square = jnp.concatenate([stacked, jnp.zeros((96, 128), F32)], axis=0).T
    out_ref[...] = square[:32, :32]


def to_next(value, axes, by):
    size = lax.axis_size(axes)
    pairs = [(i, i + by) for i in range(size) if 0 <= i + by < size]
    return lax.ppermute(value, axes, pairs)


def swapped(value):
    return lax.ppermute(value, "ctx_2", [(0, 1), (1, 0)])


def exchange(value, axes):
    return lax.all_to_all(value, axes, split_axis=0, concat_axis=0, tiled=True)


def shards(inputs, values, w_qk, conv_qk, conv_v, d_attn):
    tokens, own_values = inputs[0], values[0]
    depth = tokens.shape[1]
    splits = lax.axis_size("fsdp")
    lines = lax.axis_size("ctx_0")
    blocks = lax.axis_size(SLAB)
    peers = lax.axis_size(CTX_BATCH)
    deep = w_qk.shape[0]
    chips = lax.axis_size(CHIPS)
    place = lax.axis_index("ctx_0").astype(jnp.int32).reshape(1)
    core = lax.axis_index("ctx_2").astype(jnp.int32).reshape(1)

    (turned,) = call(turn_body, [struct((splits, 2 * F, deep), BF)], w_qk)
    weights = exchange(turned, "fsdp")
    rim = to_next(jnp.concatenate([tokens[POS - 8 :], own_values[POS - 8 :]], axis=1), CTX, 1)
    rim_tokens, rim_values = rim[:, :depth], rim[:, depth:]

    value_rows, taps = call(
        values_body,
        [struct((2, E, POS), BF), struct((CONV, 2 * F, POS), F32)],
        own_values, rim_values, d_attn[0], conv_v, conv_qk,
    )
    (spread,) = call(spread_body, [struct((blocks, 96, POS), BF)], weights, tokens, rim_tokens, value_rows, taps)
    slab = exchange(spread, SLAB)
    k_rows, state = call(state_body, [struct((blocks, ROWS, POS), BF), struct((lines, 40, POS), BF)], slab)
    states = exchange(state, "ctx_0")
    before, mixed_own, q_rows = call(
        local_body,
        [
            struct((blocks, 32, ROWS), F32), struct((blocks, 32, POS), F32), struct((blocks, ROWS, POS), BF),
        ],
        slab, k_rows,
        flops=2 * blocks * POS * POS * 48,
    )
    mixed, prior, norm = call(
        mix_body,
        [struct((blocks, 32, POS), F32), struct((blocks, 32, ROWS), BF), struct((blocks, 2 * blocks, POS), BF)],
        place, states, before, slab, mixed_own, q_rows,
    )
    norms = exchange(norm, SLAB)
    att_rows, d_mixed, grad_state = call(
        norm_body,
        [struct((blocks, 32, POS), BF), struct((blocks, 32, POS), BF), struct((lines, 40, POS), BF)],
        norms, slab, mixed, q_rows,
    )
    grad_states = exchange(grad_state, "ctx_0")
    after, d_qk, d_val = call(
        back_body,
        [struct((blocks, 32, ROWS), F32), struct((blocks, 32, POS), F32), struct((blocks, 32, POS), F32)],
        slab, d_mixed, prior, q_rows,
        flops=2 * blocks * POS * POS * 144,
    )
    (parts,) = call(
        later_body,
        [struct((blocks, 128, POS), BF)],
        place, grad_states, after, slab, k_rows, d_qk, d_val, att_rows,
    )
    sent, sent_rim, parts = lax.optimization_barrier((tokens, rim_tokens, parts))
    home = exchange(parts, SLAB)
    other_tokens = swapped(sent)
    other_rim = swapped(sent_rim)
    (grad_parts,) = call(
        grad_body,
        [struct((chips, 8, 128), BF)],
        core, home, tokens, other_tokens, rim_tokens, other_rim, taps,
        flops=4 * POS * depth * 2 * F,
    )
    arrived = exchange(grad_parts, CHIPS)
    home, _ = lax.optimization_barrier((home, grad_parts))
    attended, g_val, head = call(
        return_body, [struct((POS, E), BF), struct((POS, E), F32), struct((8, E), F32)], home, conv_v
    )
    next_rows = to_next(head, CTX, -1)
    (grad_v,) = call(rim_body, [struct((POS, E), BF)], g_val, next_rows, conv_v)
    scale = float(POS * peers) ** (-0.5)
    (grad_w,) = call(lambda a, b: sum_body(a, b, scale=scale), [struct((2 * F, 2 * F), F32)], arrived)
    return (attended[None], grad_v[None], grad_w)


def solution(mesh):
    split = Mesh(
        mesh.devices.reshape(8, 4, 2, mesh.shape["fsdp"], mesh.shape["batch"]),
        ("ctx_0", "ctx_1", "ctx_2", "fsdp", "batch"),
    )
    in_specs = (
        P("batch", CTX, None),
        P("batch", CTX, "fsdp"),
        P("fsdp", None),
        P(None, "fsdp"),
        P(None, "fsdp"),
        P("batch", CTX, "fsdp"),
    )
    out_specs = (P("batch", CTX, "fsdp"), P("batch", CTX, "fsdp"), P(CTX_BATCH, "fsdp"))
    return jax.shard_map(
        shards, mesh=split, in_specs=in_specs, out_specs=out_specs, check_vma=False
    )
```

```python
import jax
import jax.numpy as jnp
from jax import lax
from jax.experimental import pallas as pl
from jax.experimental.pallas import tpu as pltpu
from jax.sharding import Mesh
from jax.sharding import PartitionSpec as P

F = 16
E = 256
CONV = 3
POS = 128
ROWS = 160
SLAB = ("ctx_1", "ctx_2")
CTX = ("ctx_0", "ctx_1", "ctx_2")
CHIPS = ("ctx_0", "ctx_1", "batch")
CTX_BATCH = ("ctx_0", "ctx_1", "ctx_2", "batch")
BF = jnp.bfloat16
F32 = jnp.float32
eps_norm = 1e-05


def nn(a, b):
    return lax.dot_general(a, b, (((1,), (0,)), ((), ())), preferred_element_type=F32)


def nt(a, b):
    return lax.dot_general(a, b, (((1,), (1,)), ((), ())), preferred_element_type=F32)


def tn(a, b):
    return lax.dot_general(a, b, (((0,), (0,)), ((), ())), preferred_element_type=F32)


def call(body, outs, *args, flops=0):
    moved = sum(a.size * a.dtype.itemsize for a in (*args, *outs))
    return pl.pallas_call(
        body,
        out_shape=outs,
        in_specs=[
            pl.BlockSpec(memory_space=pltpu.SMEM if a.dtype == jnp.int32 else pltpu.VMEM) for a in args
        ],
        out_specs=[pl.BlockSpec(memory_space=pltpu.VMEM)] * len(outs),
        cost_estimate=pl.CostEstimate(flops=flops, bytes_accessed=moved, transcendentals=0),
        compiler_params=pltpu.CompilerParams(vmem_limit_bytes=8 << 20),
    )(*args)


def struct(shape, dtype):
    return jax.ShapeDtypeStruct(shape, dtype)


def shifted(w, s):
    return w if s % F == 0 else jnp.concatenate([w[s % F :], w[: s % F]], axis=0)


def rows_of(w):
    parts = [w]
    for s in range(8):
        parts.append(w * shifted(w, s))
    parts.append(w[:8] * w[8:])
    at = lax.broadcasted_iota(jnp.int32, (8, w.shape[1]), 0)
    parts.append(jnp.where(at == 0, 1.0, 0.0).astype(F32))
    return jnp.concatenate(parts, axis=0)


def gains():
    at = lax.broadcasted_iota(jnp.int32, (1, ROWS), 1)
    quad = jnp.where(at < 2 * F, 1.0 / 32.0, 1.0 / 16.0)
    return jnp.where(at < F, 0.25, jnp.where(at < 152, quad, 1.0)).astype(F32)


def eye(size):
    row = lax.broadcasted_iota(jnp.int32, (size, size), 0)
    col = lax.broadcasted_iota(jnp.int32, (size, size), 1)
    return jnp.where(row == col, 1.0, 0.0).astype(BF)


def rows_back(w, y):
    total = 0.25 * y[:F] + (1.0 / 16.0) * w * y[F : 2 * F]
    for s in range(1, 8):
        y_s = y[F * (s + 1) : F * (s + 2)]
        total = total + (1.0 / 16.0) * (
            shifted(w, s) * y_s + shifted(w, F - s) * shifted(y_s, F - s)
        )
    y_8 = y[144:152]
    half = jnp.concatenate([w[8:] * y_8, w[:8] * y_8], axis=0)
    return total + (1.0 / 16.0) * half


def turn_body(w_ref, cqk_ref, out_ref, taps_ref):
    turned = nt(eye(w_ref.shape[1]), w_ref[...]).astype(BF)
    for part in range(out_ref.shape[0]):
        out_ref[part] = turned[32 * part : 32 * part + 32]
    width = cqk_ref.shape[1]
    row = lax.broadcasted_iota(jnp.int32, (width, width), 0)
    col = lax.broadcasted_iota(jnp.int32, (width, width), 1)
    for tap in range(CONV):
        spread = jnp.where(row == col, jnp.broadcast_to(cqk_ref[tap : tap + 1], (width, width)), 0.0)
        taps_ref[tap] = jnp.broadcast_to(jnp.sum(spread, axis=1, keepdims=True), (width, POS))


def values_body(val_ref, hval_ref, grad_ref, cv_ref, out_ref):
    v0 = val_ref[...].astype(F32)
    hv = hval_ref[...].astype(F32)
    at = lax.broadcasted_iota(jnp.int32, v0.shape, 0)
    last, before = (jnp.broadcast_to(hv[k : k + 1], v0.shape) for k in (7, 6))
    v1 = jnp.where(at == 0, last, pltpu.roll(v0, 1, 0))
    v2 = jnp.where(at == 0, before, jnp.where(at == 1, last, pltpu.roll(v0, 2, 0)))
    valued = (cv_ref[0:1] * v0 + cv_ref[1:2] * v1 + cv_ref[2:3] * v2).astype(BF)
    square = eye(E)
    out_ref[0] = nt(square, valued).astype(BF)
    out_ref[1] = nt(square, grad_ref[...]).astype(BF)


def spread_body(w_ref, tok_ref, htok_ref, turned_ref, cqk_ref, out_ref):
    parts, _, deep = w_ref.shape
    own = jnp.zeros((2 * F, POS), F32)
    rim = jnp.zeros((2 * F, htok_ref.shape[0]), F32)
    for part in range(parts):
        w = w_ref[part]
        own = own + nt(w, tok_ref[:, deep * part : deep * part + deep])
        rim = rim + nt(w, htok_ref[:, deep * part : deep * part + deep])
    x0 = own.astype(BF).astype(F32)
    h = rim.astype(BF).astype(F32)
    lane = lax.broadcasted_iota(jnp.int32, x0.shape, 1)
    last, before = (jnp.broadcast_to(h[:, k : k + 1], x0.shape) for k in (7, 6))
    x1 = jnp.where(lane == 0, last, pltpu.roll(x0, 1, 1))
    x2 = jnp.where(lane == 0, before, jnp.where(lane == 1, last, pltpu.roll(x0, 2, 1)))
    conv = (cqk_ref[0] * x0 + cqk_ref[1] * x1 + cqk_ref[2] * x2).astype(BF)
    for peer in range(out_ref.shape[0]):
        out_ref[peer, :32] = turned_ref[0, 32 * peer : 32 * peer + 32]
        out_ref[peer, 32:64] = turned_ref[1, 32 * peer : 32 * peer + 32]
        out_ref[peer, 64:] = conv


def pack(total):
    side = [total[8 * i : 8 * i + 8, POS:] for i in range(4)]
    return jnp.concatenate([total[:, :POS], jnp.concatenate(side, axis=1)], axis=0)


def unpack(packed):
    side = jnp.concatenate([packed[32:, 32 * i : 32 * i + 32] for i in range(4)], axis=0)
    return jnp.concatenate([packed[:32], side], axis=1)


def state_body(in_ref, krows_ref, out_ref):
    blocks = range(in_ref.shape[0])
    for b in blocks:
        krows_ref[b] = rows_of(in_ref[b, 80:].astype(F32)).astype(BF)
    values = jnp.concatenate([in_ref[b, :32] for b in blocks], axis=1)
    total = pack(nt(values, jnp.concatenate([krows_ref[b] for b in blocks], axis=1))).astype(BF)
    for peer in range(out_ref.shape[0]):
        out_ref[peer] = total


def scores(in_ref, b):
    row = lax.broadcasted_iota(jnp.int32, (POS, POS), 0)
    col = lax.broadcasted_iota(jnp.int32, (POS, POS), 1)
    dotted = tn(in_ref[b, 80:], in_ref[b, 64:80]) * 0.25
    causal = row <= col
    return dotted, causal, jnp.where(causal, 1.0 + dotted + 0.5 * dotted * dotted, 0.0).astype(BF)


def local_body(in_ref, krows_ref, before_ref, mixed_ref, qrows_ref):
    total = jnp.zeros((32, ROWS), F32)
    for b in range(in_ref.shape[0]):
        before_ref[b] = total
        total = total + nt(in_ref[b, :32], krows_ref[b])
        mixed_ref[b] = nn(in_ref[b, :32], scores(in_ref, b)[2])
        qrows_ref[b] = rows_of(in_ref[b, 64:80].astype(F32)).astype(BF)


def mix_body(at_ref, sums_ref, before_ref, in_ref, local_ref, qrows_ref, mixed_ref, prior_ref, out_ref):
    at = at_ref[0]
    total = jnp.zeros(sums_ref.shape[1:], F32)
    for x in range(sums_ref.shape[0]):
        total = total + jnp.where(x < at, sums_ref[x].astype(F32), 0.0)
    total = unpack(total)
    gain = gains()
    squares, products = [], []
    for b in range(in_ref.shape[0]):
        prior = before_ref[b] + total
        prior_ref[b] = prior.astype(BF)
        mixed = local_ref[b] + nn((prior * gain).astype(BF), qrows_ref[b])
        mixed_ref[b] = mixed
        squares.append(jnp.sum(mixed * mixed, axis=0, keepdims=True))
        products.append(jnp.sum(in_ref[b, 32:64].astype(F32) * mixed, axis=0, keepdims=True))
    rows = jnp.concatenate(squares + products, axis=0).astype(BF)
    for peer in range(out_ref.shape[0]):
        out_ref[peer] = rows


def norm_body(sums_ref, in_ref, mixed_ref, qrows_ref, att_ref, dmix_ref, out_ref):
    rows = sums_ref[0].astype(F32)
    for peer in range(1, sums_ref.shape[0]):
        rows = rows + sums_ref[peer].astype(F32)
    rows = rows * (1.0 / E)
    blocks = in_ref.shape[0]
    for b in range(blocks):
        inv = lax.rsqrt(rows[b : b + 1] + eps_norm)
        normed = mixed_ref[b] * inv
        att_ref[b] = normed.astype(BF)
        grad = in_ref[b, 32:64].astype(F32)
        d_mixed = inv * (grad - normed * (inv * rows[blocks + b : blocks + b + 1]))
        dmix_ref[b] = d_mixed.astype(BF)
    d_all = jnp.concatenate([dmix_ref[b] for b in range(blocks)], axis=1)
    total = pack(nt(d_all, jnp.concatenate([qrows_ref[b] for b in range(blocks)], axis=1))).astype(BF)
    for peer in range(out_ref.shape[0]):
        out_ref[peer] = total


def back_body(in_ref, dmix_ref, prior_ref, qrows_ref, after_ref, dqk_ref, dval_ref):
    total = jnp.zeros((32, ROWS), F32)
    for b in reversed(range(in_ref.shape[0])):
        after_ref[b] = total
        total = total + nt(dmix_ref[b], qrows_ref[b])
        queries, keys = in_ref[b, 64:80], in_ref[b, 80:]
        d_mixed = dmix_ref[b]
        dotted, causal, kernel = scores(in_ref, b)
        slope = jnp.where(causal, (1.0 + dotted) * 0.25, 0.0)
        d_score = (tn(in_ref[b, :32], d_mixed) * slope).astype(BF)
        dqk_ref[b, :F] = nn(keys, d_score) + rows_back(queries.astype(F32), tn(prior_ref[b], d_mixed))
        dqk_ref[b, F:] = nt(queries, d_score)
        dval_ref[b] = nt(d_mixed, kernel)


def later_body(at_ref, sums_ref, after_ref, in_ref, krows_ref, dqk_ref, dval_ref, att_ref, out_ref):
    at = at_ref[0]
    total = jnp.zeros(sums_ref.shape[1:], F32)
    for x in range(sums_ref.shape[0]):
        total = total + jnp.where(x > at, sums_ref[x].astype(F32), 0.0)
    total = unpack(total)
    gain = gains()
    for b in range(in_ref.shape[0]):
        later = after_ref[b] + total
        keys = in_ref[b, 80:].astype(F32)
        d_key = dqk_ref[b, F:] + rows_back(keys, tn(later.astype(BF), in_ref[b, :32]))
        part = jnp.concatenate([dqk_ref[b, :F], d_key], axis=0).astype(BF)
        first, at_row = b - b % 2, 32 * (b % 2)
        out_ref[first, at_row : at_row + 32] = part
        out_ref[first + 1, at_row : at_row + 32] = part
        out_ref[b, 64:96] = att_ref[b]
        out_ref[b, 96:] = (dval_ref[b] + nn((later * gain).astype(BF), krows_ref[b])).astype(BF)


def halves_body(core_ref, tok_ref, htok_ref, mine_ref, theirs_ref):
    for refs, wanted in (((mine_ref, theirs_ref), 0), ((theirs_ref, mine_ref), 1)):

        @pl.when(core_ref[0] == wanted)
        def _(refs=refs):
            for in_ref, at in ((tok_ref, slice(0, POS)), (htok_ref, slice(POS, POS + 8))):
                for m in range(in_ref.shape[1] // 256):
                    left = in_ref[:, 256 * m : 256 * m + 128]
                    right = in_ref[:, 256 * m + 128 : 256 * m + 256]
                    cols = slice(128 * m, 128 * m + 128)
                    refs[0][at, cols] = jnp.concatenate([left[:, :64], right[:, :64]], axis=1)
                    refs[1][at, cols] = jnp.concatenate([left[:, 64:], right[:, 64:]], axis=1)


def grad_body(core_ref, sums_ref, tok_ref, other_ref, cqk_ref, out_ref):
    pair = sums_ref[0, : 4 * F].astype(F32)
    for peer in range(1, sums_ref.shape[0]):
        pair = pair + sums_ref[peer, : 4 * F].astype(F32)
    first, second = pair[: 2 * F], pair[2 * F :]
    core = core_ref[0]
    lane = lax.broadcasted_iota(jnp.int32, first.shape, 1)

    def ahead(d, nxt, by):
        return jnp.where(lane < POS - by, pltpu.roll(d, POS - by, 1), pltpu.roll(nxt, POS - by, 1))

    zero = jnp.zeros_like(first)
    of_first = cqk_ref[0] * first + cqk_ref[1] * ahead(first, second, 1) + cqk_ref[2] * ahead(first, second, 2)
    of_second = cqk_ref[0] * second + cqk_ref[1] * ahead(second, zero, 1) + cqk_ref[2] * ahead(second, zero, 2)
    to_last = pltpu.roll(cqk_ref[2] * first, 6, 1)
    near = pltpu.roll(cqk_ref[1] * first, 7, 1) + to_last
    rim = jnp.where(lane == 6, to_last, jnp.where(lane == 7, near, 0.0))[:, :8]
    own_b = jnp.where(core == 0, of_first, of_second).astype(BF)
    other_b = jnp.where(core == 0, of_second, of_first).astype(BF)
    rim_own = jnp.where(core == 0, rim, 0.0).astype(BF)
    rim_other = jnp.where(core == 0, 0.0, rim).astype(BF)

    group = lax.broadcasted_iota(jnp.int32, (8, 128), 1) // 32
    chunk = 512
    for start in range(0, tok_ref.shape[1], chunk):
        at = slice(start, start + chunk)
        part = nn(own_b, tok_ref[:POS, at]) + nn(other_b, other_ref[:POS, at])
        part = part + nn(rim_own, tok_ref[POS:, at]) + nn(rim_other, other_ref[POS:, at])
        for at_lane in range(0, chunk, 128):
            blocks = [part[8 * i : 8 * i + 8, at_lane : at_lane + 128] for i in range(4)]
            for q in range(4):
                moved = [pltpu.roll(b, 32 * ((i - q) % 4), 1) if i != q else b for i, b in enumerate(blocks)]
                packed = jnp.where(
                    group == 0, moved[0], jnp.where(group == 1, moved[1], jnp.where(group == 2, moved[2], moved[3]))
                )
                out_ref[(start + at_lane) // 32 + q] = packed.astype(out_ref.dtype)


def return_body(in_ref, cv_ref, att_ref, gval_ref, head_ref):
    square = eye(POS)
    peers = range(in_ref.shape[0])
    att = jnp.concatenate([in_ref[j, 64:96] for j in peers], axis=0)
    d_rows = jnp.concatenate([in_ref[j, 96:] for j in peers], axis=0)
    att_ref[...] = nt(square, att).astype(BF)
    dv = nt(square, d_rows)
    head_ref[...] = dv[:8]
    at = lax.broadcasted_iota(jnp.int32, dv.shape, 0)
    gval = cv_ref[0:1] * dv
    gval = gval + cv_ref[1:2] * jnp.where(at < POS - 1, pltpu.roll(dv, POS - 1, 0), 0.0)
    gval = gval + cv_ref[2:3] * jnp.where(at < POS - 2, pltpu.roll(dv, POS - 2, 0), 0.0)
    gval_ref[...] = gval


def rim_body(gval_ref, next_ref, cv_ref, out_ref):
    out_ref[...] = gval_ref[...].astype(BF)
    nxt = next_ref[...]
    at = lax.broadcasted_iota(jnp.int32, nxt.shape, 0)
    c1, c2 = cv_ref[1:2], cv_ref[2:3]
    first, second = (jnp.broadcast_to(nxt[k : k + 1], nxt.shape) for k in (0, 1))
    more = jnp.where(at == 6, c2 * first, jnp.where(at == 7, c1 * first + c2 * second, 0.0))
    out_ref[POS - 8 :] = (gval_ref[POS - 8 :] + more).astype(BF)


def sum_body(parts_ref, out_ref, *, scale):
    totals = [parts_ref[k].astype(F32) for k in range(8)]
    for k in range(8, parts_ref.shape[0]):
        totals[k % 8] = totals[k % 8] + parts_ref[k].astype(F32)
    while len(totals) > 1:
        totals = [a + b for a, b in zip(totals[::2], totals[1::2])]
    total = totals[0] * scale
    stacked = jnp.concatenate([total] + [pltpu.roll(total, 128 - 32 * i, 1) for i in (1, 2, 3)], axis=0)
    square = jnp.concatenate([stacked, jnp.zeros((96, 128), F32)], axis=0).T
    out_ref[...] = square[:32, :32]


def to_next(value, axes, by):
    size = lax.axis_size(axes)
    pairs = [(i, i + by) for i in range(size) if 0 <= i + by < size]
    return lax.ppermute(value, axes, pairs)


def swapped(value):
    return lax.ppermute(value, "ctx_2", [(0, 1), (1, 0)])


def exchange(value, axes):
    return lax.all_to_all(value, axes, split_axis=0, concat_axis=0, tiled=True)


def shards(inputs, values, w_qk, conv_qk, conv_v, d_attn):
    tokens, own_values = inputs[0], values[0]
    depth = tokens.shape[1]
    splits = lax.axis_size("fsdp")
    lines = lax.axis_size("ctx_0")
    blocks = lax.axis_size(SLAB)
    peers = lax.axis_size(CTX_BATCH)
    deep = w_qk.shape[0]
    chips = lax.axis_size(CHIPS)
    place = lax.axis_index("ctx_0").astype(jnp.int32).reshape(1)
    core = lax.axis_index("ctx_2").astype(jnp.int32).reshape(1)

    turned, taps = call(
        turn_body,
        [struct((splits, 2 * F, deep), BF), struct((CONV, 2 * F, POS), F32)],
        w_qk, conv_qk,
    )
    weights = exchange(turned, "fsdp")
    rim = to_next(jnp.concatenate([tokens[POS - 8 :], own_values[POS - 8 :]], axis=1), CTX, 1)
    rim_tokens, rim_values = rim[:, :depth], rim[:, depth:]

    (value_rows,) = call(values_body, [struct((2, E, POS), BF)], own_values, rim_values, d_attn[0], conv_v)
    (spread,) = call(spread_body, [struct((blocks, 96, POS), BF)], weights, tokens, rim_tokens, value_rows, taps)
    whole, rim_tokens, spread = lax.optimization_barrier((tokens, rim_tokens, spread))
    slab = exchange(spread, SLAB)
    half = struct((POS + 8, depth // 2), BF)
    own_half, sent = call(halves_body, [half, half], core, whole, rim_tokens)
    other_half = swapped(sent)
    slab, other_half = lax.optimization_barrier((slab, other_half))
    k_rows, state = call(state_body, [struct((blocks, ROWS, POS), BF), struct((lines, 40, POS), BF)], slab)
    states = exchange(state, "ctx_0")
    before, mixed_own, q_rows = call(
        local_body,
        [
            struct((blocks, 32, ROWS), F32), struct((blocks, 32, POS), F32), struct((blocks, ROWS, POS), BF),
        ],
        slab, k_rows,
        flops=2 * blocks * POS * POS * 48,
    )
    mixed, prior, norm = call(
        mix_body,
        [struct((blocks, 32, POS), F32), struct((blocks, 32, ROWS), BF), struct((blocks, 2 * blocks, POS), BF)],
        place, states, before, slab, mixed_own, q_rows,
    )
    norms = exchange(norm, SLAB)
    att_rows, d_mixed, grad_state = call(
        norm_body,
        [struct((blocks, 32, POS), BF), struct((blocks, 32, POS), BF), struct((lines, 40, POS), BF)],
        norms, slab, mixed, q_rows,
    )
    grad_states = exchange(grad_state, "ctx_0")
    after, d_qk, d_val = call(
        back_body,
        [struct((blocks, 32, ROWS), F32), struct((blocks, 32, POS), F32), struct((blocks, 32, POS), F32)],
        slab, d_mixed, prior, q_rows,
        flops=2 * blocks * POS * POS * 144,
    )
    (parts,) = call(
        later_body,
        [struct((blocks, 128, POS), BF)],
        place, grad_states, after, slab, k_rows, d_qk, d_val, att_rows,
    )
    home = exchange(parts, SLAB)
    (grad_parts,) = call(
        grad_body,
        [struct((chips, 8, 128), BF)],
        core, home, own_half, other_half, taps,
        flops=2 * POS * depth * 2 * F,
    )
    arrived = exchange(grad_parts, CHIPS)
    home, _ = lax.optimization_barrier((home, grad_parts))
    attended, g_val, head = call(
        return_body, [struct((POS, E), BF), struct((POS, E), F32), struct((8, E), F32)], home, conv_v
    )
    next_rows = to_next(head, CTX, -1)
    (grad_v,) = call(rim_body, [struct((POS, E), BF)], g_val, next_rows, conv_v)
    scale = float(POS * peers) ** (-0.5)
    (grad_w,) = call(lambda a, b: sum_body(a, b, scale=scale), [struct((2 * F, 2 * F), F32)], arrived)
    return (attended[None], grad_v[None], grad_w)


def solution(mesh):
    split = Mesh(
        mesh.devices.reshape(8, 4, 2, mesh.shape["fsdp"], mesh.shape["batch"]),
        ("ctx_0", "ctx_1", "ctx_2", "fsdp", "batch"),
    )
    in_specs = (
        P("batch", CTX, None),
        P("batch", CTX, "fsdp"),
        P("fsdp", None),
        P(None, "fsdp"),
        P(None, "fsdp"),
        P("batch", CTX, "fsdp"),
    )
    out_specs = (P("batch", CTX, "fsdp"), P("batch", CTX, "fsdp"), P(CTX_BATCH, "fsdp"))
    return jax.shard_map(
        shards, mesh=split, in_specs=in_specs, out_specs=out_specs, check_vma=False
    )
```

```python
import jax
import jax.numpy as jnp
from jax import lax
from jax.experimental import pallas as pl
from jax.experimental.pallas import tpu as pltpu
from jax.sharding import Mesh
from jax.sharding import PartitionSpec as P

F = 16
E = 256
CONV = 3
POS = 128
ROWS = 160
SLAB = ("ctx_1", "ctx_2")
CTX = ("ctx_0", "ctx_1", "ctx_2")
CHIPS = ("ctx_0", "ctx_1", "batch")
CTX_BATCH = ("ctx_0", "ctx_1", "ctx_2", "batch")
BF = jnp.bfloat16
F32 = jnp.float32
eps_norm = 1e-05


def nn(a, b):
    return lax.dot_general(a, b, (((1,), (0,)), ((), ())), preferred_element_type=F32)


def nt(a, b):
    return lax.dot_general(a, b, (((1,), (1,)), ((), ())), preferred_element_type=F32)


def tn(a, b):
    return lax.dot_general(a, b, (((0,), (0,)), ((), ())), preferred_element_type=F32)


def call(body, outs, *args, flops=0):
    moved = sum(a.size * a.dtype.itemsize for a in (*args, *outs))
    return pl.pallas_call(
        body,
        out_shape=outs,
        in_specs=[
            pl.BlockSpec(memory_space=pltpu.SMEM if a.dtype == jnp.int32 else pltpu.VMEM) for a in args
        ],
        out_specs=[pl.BlockSpec(memory_space=pltpu.VMEM)] * len(outs),
        cost_estimate=pl.CostEstimate(flops=flops, bytes_accessed=moved, transcendentals=0),
        compiler_params=pltpu.CompilerParams(vmem_limit_bytes=8 << 20),
    )(*args)


def struct(shape, dtype):
    return jax.ShapeDtypeStruct(shape, dtype)


def shifted(w, s):
    return w if s % F == 0 else jnp.concatenate([w[s % F :], w[: s % F]], axis=0)


def rows_of(w):
    parts = [w]
    for s in range(8):
        parts.append(w * shifted(w, s))
    parts.append(w[:8] * w[8:])
    at = lax.broadcasted_iota(jnp.int32, (8, w.shape[1]), 0)
    parts.append(jnp.where(at == 0, 1.0, 0.0).astype(F32))
    return jnp.concatenate(parts, axis=0)


def gains():
    at = lax.broadcasted_iota(jnp.int32, (1, ROWS), 1)
    quad = jnp.where(at < 2 * F, 1.0 / 32.0, 1.0 / 16.0)
    return jnp.where(at < F, 0.25, jnp.where(at < 152, quad, 1.0)).astype(F32)


def eye(size):
    row = lax.broadcasted_iota(jnp.int32, (size, size), 0)
    col = lax.broadcasted_iota(jnp.int32, (size, size), 1)
    return jnp.where(row == col, 1.0, 0.0).astype(BF)


def rows_back(w, y):
    total = 0.25 * y[:F] + (1.0 / 16.0) * w * y[F : 2 * F]
    for s in range(1, 8):
        y_s = y[F * (s + 1) : F * (s + 2)]
        total = total + (1.0 / 16.0) * (
            shifted(w, s) * y_s + shifted(w, F - s) * shifted(y_s, F - s)
        )
    y_8 = y[144:152]
    half = jnp.concatenate([w[8:] * y_8, w[:8] * y_8], axis=0)
    return total + (1.0 / 16.0) * half


def turn_body(w_hbm, cqk_hbm, tok_hbm, val_hbm, grad_hbm, cv_hbm, out_ref, rim_ref, val_ref, grad_ref, w_buf, cqk_buf, val_buf, sems):
    depth = tok_hbm.shape[1]
    pairs = (
        (w_hbm, w_buf),
        (cqk_hbm, cqk_buf),
        (tok_hbm.at[POS - 8 :], rim_ref.at[:, :depth]),
        (val_hbm.at[POS - 8 :], rim_ref.at[:, depth:]),
        (val_hbm, val_buf),
        (grad_hbm, grad_ref),
        (cv_hbm, val_ref.at[POS : POS + CONV]),
    )
    copies = [pltpu.make_async_copy(source, target, sems.at[k]) for k, (source, target) in enumerate(pairs)]
    for copy in copies:
        copy.start()
    copies[0].wait()
    turned = nt(eye(w_buf.shape[1]), w_buf[...]).astype(BF)
    for part in range(out_ref.shape[0]):
        out_ref[part] = turned[32 * part : 32 * part + 32]
    copies[1].wait()
    width = cqk_buf.shape[1]
    row = lax.broadcasted_iota(jnp.int32, (width, width), 0)
    col = lax.broadcasted_iota(jnp.int32, (width, width), 1)
    for tap in range(CONV):
        spread = jnp.where(row == col, jnp.broadcast_to(cqk_buf[tap : tap + 1], (width, width)), 0.0)
        at = POS + 8 + width * tap
        val_ref[at : at + width, :POS] = jnp.broadcast_to(jnp.sum(spread, axis=1, keepdims=True), (width, POS))
    for copy in copies[2:]:
        copy.wait()
    val_ref[:POS] = val_buf[...].astype(F32)


def values_body(val_ref, hval_ref, grad_ref, out_ref, taps_ref):
    for tap in range(CONV):
        at = POS + 8 + 2 * F * tap
        taps_ref[tap] = val_ref[at : at + 2 * F, :POS]
    v0 = val_ref[:POS]
    first, second, third = (val_ref[POS + k : POS + k + 1] for k in range(CONV))
    hv = hval_ref[...].astype(F32)
    at = lax.broadcasted_iota(jnp.int32, v0.shape, 0)
    last, before = (jnp.broadcast_to(hv[k : k + 1], v0.shape) for k in (7, 6))
    v1 = jnp.where(at == 0, last, pltpu.roll(v0, 1, 0))
    v2 = jnp.where(at == 0, before, jnp.where(at == 1, last, pltpu.roll(v0, 2, 0)))
    valued = (first * v0 + second * v1 + third * v2).astype(BF)
    square = eye(E)
    out_ref[0] = nt(square, valued).astype(BF)
    out_ref[1] = nt(square, grad_ref[...]).astype(BF)


def spread_body(w_ref, tok_ref, htok_ref, turned_ref, cqk_ref, out_ref):
    parts, _, deep = w_ref.shape
    own = jnp.zeros((2 * F, POS), F32)
    rim = jnp.zeros((2 * F, htok_ref.shape[0]), F32)
    for part in range(parts):
        w = w_ref[part]
        own = own + nt(w, tok_ref[:, deep * part : deep * part + deep])
        rim = rim + nt(w, htok_ref[:, deep * part : deep * part + deep])
    x0 = own.astype(BF).astype(F32)
    h = rim.astype(BF).astype(F32)
    lane = lax.broadcasted_iota(jnp.int32, x0.shape, 1)
    last, before = (jnp.broadcast_to(h[:, k : k + 1], x0.shape) for k in (7, 6))
    x1 = jnp.where(lane == 0, last, pltpu.roll(x0, 1, 1))
    x2 = jnp.where(lane == 0, before, jnp.where(lane == 1, last, pltpu.roll(x0, 2, 1)))
    conv = (cqk_ref[0] * x0 + cqk_ref[1] * x1 + cqk_ref[2] * x2).astype(BF)
    for peer in range(out_ref.shape[0]):
        out_ref[peer, :32] = turned_ref[0, 32 * peer : 32 * peer + 32]
        out_ref[peer, 32:64] = turned_ref[1, 32 * peer : 32 * peer + 32]
        out_ref[peer, 64:] = conv


def pack(total):
    side = [total[8 * i : 8 * i + 8, POS:] for i in range(4)]
    return jnp.concatenate([total[:, :POS], jnp.concatenate(side, axis=1)], axis=0)


def unpack(packed):
    side = jnp.concatenate([packed[32:, 32 * i : 32 * i + 32] for i in range(4)], axis=0)
    return jnp.concatenate([packed[:32], side], axis=1)


def state_body(in_ref, krows_ref, out_ref):
    blocks = range(in_ref.shape[0])
    for b in blocks:
        krows_ref[b] = rows_of(in_ref[b, 80:].astype(F32)).astype(BF)
    values = jnp.concatenate([in_ref[b, :32] for b in blocks], axis=1)
    total = pack(nt(values, jnp.concatenate([krows_ref[b] for b in blocks], axis=1))).astype(BF)
    for peer in range(out_ref.shape[0]):
        out_ref[peer] = total


def scores(in_ref, b):
    row = lax.broadcasted_iota(jnp.int32, (POS, POS), 0)
    col = lax.broadcasted_iota(jnp.int32, (POS, POS), 1)
    dotted = tn(in_ref[b, 80:], in_ref[b, 64:80]) * 0.25
    causal = row <= col
    return dotted, causal, jnp.where(causal, 1.0 + dotted + 0.5 * dotted * dotted, 0.0).astype(BF)


def local_body(in_ref, krows_ref, before_ref, mixed_ref, qrows_ref):
    total = jnp.zeros((32, ROWS), F32)
    for b in range(in_ref.shape[0]):
        before_ref[b] = total
        total = total + nt(in_ref[b, :32], krows_ref[b])
        mixed_ref[b] = nn(in_ref[b, :32], scores(in_ref, b)[2])
        qrows_ref[b] = rows_of(in_ref[b, 64:80].astype(F32)).astype(BF)


def mix_body(at_ref, sums_ref, before_ref, in_ref, local_ref, qrows_ref, mixed_ref, prior_ref, out_ref):
    at = at_ref[0]
    total = jnp.zeros(sums_ref.shape[1:], F32)
    for x in range(sums_ref.shape[0]):
        total = total + jnp.where(x < at, sums_ref[x].astype(F32), 0.0)
    total = unpack(total)
    gain = gains()
    squares, products = [], []
    for b in range(in_ref.shape[0]):
        prior = before_ref[b] + total
        prior_ref[b] = prior.astype(BF)
        mixed = local_ref[b] + nn((prior * gain).astype(BF), qrows_ref[b])
        mixed_ref[b] = mixed
        squares.append(jnp.sum(mixed * mixed, axis=0, keepdims=True))
        products.append(jnp.sum(in_ref[b, 32:64].astype(F32) * mixed, axis=0, keepdims=True))
    rows = jnp.concatenate(squares + products, axis=0).astype(BF)
    for peer in range(out_ref.shape[0]):
        out_ref[peer] = rows


def norm_body(sums_ref, in_ref, mixed_ref, qrows_ref, att_ref, dmix_ref, out_ref):
    rows = sums_ref[0].astype(F32)
    for peer in range(1, sums_ref.shape[0]):
        rows = rows + sums_ref[peer].astype(F32)
    rows = rows * (1.0 / E)
    blocks = in_ref.shape[0]
    for b in range(blocks):
        inv = lax.rsqrt(rows[b : b + 1] + eps_norm)
        normed = mixed_ref[b] * inv
        att_ref[b] = normed.astype(BF)
        grad = in_ref[b, 32:64].astype(F32)
        d_mixed = inv * (grad - normed * (inv * rows[blocks + b : blocks + b + 1]))
        dmix_ref[b] = d_mixed.astype(BF)
    d_all = jnp.concatenate([dmix_ref[b] for b in range(blocks)], axis=1)
    total = pack(nt(d_all, jnp.concatenate([qrows_ref[b] for b in range(blocks)], axis=1))).astype(BF)
    for peer in range(out_ref.shape[0]):
        out_ref[peer] = total


def back_body(in_ref, dmix_ref, prior_ref, qrows_ref, after_ref, dqk_ref, dval_ref):
    total = jnp.zeros((32, ROWS), F32)
    for b in reversed(range(in_ref.shape[0])):
        after_ref[b] = total
        total = total + nt(dmix_ref[b], qrows_ref[b])
        queries, keys = in_ref[b, 64:80], in_ref[b, 80:]
        d_mixed = dmix_ref[b]
        dotted, causal, kernel = scores(in_ref, b)
        slope = jnp.where(causal, (1.0 + dotted) * 0.25, 0.0)
        d_score = (tn(in_ref[b, :32], d_mixed) * slope).astype(BF)
        dqk_ref[b, :F] = nn(keys, d_score) + rows_back(queries.astype(F32), tn(prior_ref[b], d_mixed))
        dqk_ref[b, F:] = nt(queries, d_score)
        dval_ref[b] = nt(d_mixed, kernel)


def later_body(at_ref, sums_ref, after_ref, in_ref, krows_ref, dqk_ref, dval_ref, att_ref, out_ref):
    at = at_ref[0]
    total = jnp.zeros(sums_ref.shape[1:], F32)
    for x in range(sums_ref.shape[0]):
        total = total + jnp.where(x > at, sums_ref[x].astype(F32), 0.0)
    total = unpack(total)
    gain = gains()
    for b in range(in_ref.shape[0]):
        later = after_ref[b] + total
        keys = in_ref[b, 80:].astype(F32)
        d_key = dqk_ref[b, F:] + rows_back(keys, tn(later.astype(BF), in_ref[b, :32]))
        part = jnp.concatenate([dqk_ref[b, :F], d_key], axis=0).astype(BF)
        first, at_row = b - b % 2, 32 * (b % 2)
        out_ref[first, at_row : at_row + 32] = part
        out_ref[first + 1, at_row : at_row + 32] = part
        out_ref[b, 64:96] = att_ref[b]
        out_ref[b, 96:] = (dval_ref[b] + nn((later * gain).astype(BF), krows_ref[b])).astype(BF)


def halves_body(core_ref, tok_ref, htok_ref, mine_ref, theirs_ref):
    for refs, wanted in (((mine_ref, theirs_ref), 0), ((theirs_ref, mine_ref), 1)):

        @pl.when(core_ref[0] == wanted)
        def _(refs=refs):
            for in_ref, at in ((tok_ref, slice(0, POS)), (htok_ref, slice(POS, POS + 8))):
                for m in range(in_ref.shape[1] // 256):
                    left = in_ref[:, 256 * m : 256 * m + 128]
                    right = in_ref[:, 256 * m + 128 : 256 * m + 256]
                    cols = slice(128 * m, 128 * m + 128)
                    refs[0][at, cols] = jnp.concatenate([left[:, :64], right[:, :64]], axis=1)
                    refs[1][at, cols] = jnp.concatenate([left[:, 64:], right[:, 64:]], axis=1)


def grad_body(core_ref, sums_ref, tok_ref, other_ref, cqk_ref, out_ref):
    pair = sums_ref[0, : 4 * F].astype(F32)
    for peer in range(1, sums_ref.shape[0]):
        pair = pair + sums_ref[peer, : 4 * F].astype(F32)
    first, second = pair[: 2 * F], pair[2 * F :]
    core = core_ref[0]
    lane = lax.broadcasted_iota(jnp.int32, first.shape, 1)

    def ahead(d, nxt, by):
        return jnp.where(lane < POS - by, pltpu.roll(d, POS - by, 1), pltpu.roll(nxt, POS - by, 1))

    zero = jnp.zeros_like(first)
    of_first = cqk_ref[0] * first + cqk_ref[1] * ahead(first, second, 1) + cqk_ref[2] * ahead(first, second, 2)
    of_second = cqk_ref[0] * second + cqk_ref[1] * ahead(second, zero, 1) + cqk_ref[2] * ahead(second, zero, 2)
    to_last = pltpu.roll(cqk_ref[2] * first, 6, 1)
    near = pltpu.roll(cqk_ref[1] * first, 7, 1) + to_last
    rim = jnp.where(lane == 6, to_last, jnp.where(lane == 7, near, 0.0))[:, :8]
    own_b = jnp.where(core == 0, of_first, of_second).astype(BF)
    other_b = jnp.where(core == 0, of_second, of_first).astype(BF)
    rim_own = jnp.where(core == 0, rim, 0.0).astype(BF)
    rim_other = jnp.where(core == 0, 0.0, rim).astype(BF)

    group = lax.broadcasted_iota(jnp.int32, (8, 128), 1) // 32
    chunk = 512
    for start in range(0, tok_ref.shape[1], chunk):
        at = slice(start, start + chunk)
        part = nn(own_b, tok_ref[:POS, at]) + nn(other_b, other_ref[:POS, at])
        part = part + nn(rim_own, tok_ref[POS:, at]) + nn(rim_other, other_ref[POS:, at])
        for at_lane in range(0, chunk, 128):
            blocks = [part[8 * i : 8 * i + 8, at_lane : at_lane + 128] for i in range(4)]
            for q in range(4):
                moved = [pltpu.roll(b, 32 * ((i - q) % 4), 1) if i != q else b for i, b in enumerate(blocks)]
                packed = jnp.where(
                    group == 0, moved[0], jnp.where(group == 1, moved[1], jnp.where(group == 2, moved[2], moved[3]))
                )
                out_ref[(start + at_lane) // 32 + q] = packed.astype(out_ref.dtype)


def return_body(in_ref, cv_ref, att_ref, gval_ref, head_ref):
    square = eye(POS)
    peers = range(in_ref.shape[0])
    att = jnp.concatenate([in_ref[j, 64:96] for j in peers], axis=0)
    d_rows = jnp.concatenate([in_ref[j, 96:] for j in peers], axis=0)
    att_ref[...] = nt(square, att).astype(BF)
    dv = nt(square, d_rows)
    head_ref[...] = dv[:8]
    at = lax.broadcasted_iota(jnp.int32, dv.shape, 0)
    gval = cv_ref[0:1] * dv
    gval = gval + cv_ref[1:2] * jnp.where(at < POS - 1, pltpu.roll(dv, POS - 1, 0), 0.0)
    gval = gval + cv_ref[2:3] * jnp.where(at < POS - 2, pltpu.roll(dv, POS - 2, 0), 0.0)
    gval_ref[...] = gval


def rim_body(gval_ref, next_ref, cv_ref, out_ref):
    out_ref[...] = gval_ref[...].astype(BF)
    nxt = next_ref[...]
    at = lax.broadcasted_iota(jnp.int32, nxt.shape, 0)
    c1, c2 = cv_ref[1:2], cv_ref[2:3]
    first, second = (jnp.broadcast_to(nxt[k : k + 1], nxt.shape) for k in (0, 1))
    more = jnp.where(at == 6, c2 * first, jnp.where(at == 7, c1 * first + c2 * second, 0.0))
    out_ref[POS - 8 :] = (gval_ref[POS - 8 :] + more).astype(BF)


def sum_body(parts_ref, out_ref, *, scale):
    totals = [parts_ref[k].astype(F32) for k in range(8)]
    for k in range(8, parts_ref.shape[0]):
        totals[k % 8] = totals[k % 8] + parts_ref[k].astype(F32)
    while len(totals) > 1:
        totals = [a + b for a, b in zip(totals[::2], totals[1::2])]
    total = totals[0] * scale
    stacked = jnp.concatenate([total] + [pltpu.roll(total, 128 - 32 * i, 1) for i in (1, 2, 3)], axis=0)
    square = jnp.concatenate([stacked, jnp.zeros((96, 128), F32)], axis=0).T
    out_ref[...] = square[:32, :32]


def to_next(value, axes, by):
    size = lax.axis_size(axes)
    pairs = [(i, i + by) for i in range(size) if 0 <= i + by < size]
    return lax.ppermute(value, axes, pairs)


def swapped(value):
    return lax.ppermute(value, "ctx_2", [(0, 1), (1, 0)])


def exchange(value, axes):
    return lax.all_to_all(value, axes, split_axis=0, concat_axis=0, tiled=True)


def shards(inputs, values, w_qk, conv_qk, conv_v, d_attn):
    tokens, own_values = inputs[0], values[0]
    depth = tokens.shape[1]
    splits = lax.axis_size("fsdp")
    lines = lax.axis_size("ctx_0")
    blocks = lax.axis_size(SLAB)
    peers = lax.axis_size(CTX_BATCH)
    deep = w_qk.shape[0]
    chips = lax.axis_size(CHIPS)
    place = lax.axis_index("ctx_0").astype(jnp.int32).reshape(1)
    core = lax.axis_index("ctx_2").astype(jnp.int32).reshape(1)

    sources = (w_qk, conv_qk, tokens, own_values, d_attn[0], conv_v)
    fetched = [
        struct((splits, 2 * F, deep), BF), struct((8, depth + E), BF),
        struct((POS + 8 + CONV * 2 * F, E), F32), struct((POS, E), BF),
    ]
    turned, rim, own_values, own_grad = pl.pallas_call(
        turn_body,
        out_shape=fetched,
        in_specs=[pl.BlockSpec(memory_space=pltpu.HBM)] * len(sources),
        out_specs=[pl.BlockSpec(memory_space=pltpu.VMEM)] * len(fetched),
        scratch_shapes=[
            pltpu.VMEM(w_qk.shape, BF), pltpu.VMEM(conv_qk.shape, F32), pltpu.VMEM((POS, E), BF), pltpu.SemaphoreType.DMA((7,))
        ],
        compiler_params=pltpu.CompilerParams(vmem_limit_bytes=60 * 1024 * 1024),
        name="turn",
    )(*sources)
    weights = exchange(turned, "fsdp")
    rim = to_next(rim, CTX, 1)
    rim_tokens, rim_values = rim[:, :depth], rim[:, depth:]

    value_rows, taps = call(
        values_body,
        [struct((2, E, POS), BF), struct((CONV, 2 * F, POS), F32)],
        own_values, rim_values, own_grad,
    )
    (spread,) = call(spread_body, [struct((blocks, 96, POS), BF)], weights, tokens, rim_tokens, value_rows, taps)
    whole, rim_tokens, spread = lax.optimization_barrier((tokens, rim_tokens, spread))
    slab = exchange(spread, SLAB)
    half = struct((POS + 8, depth // 2), BF)
    own_half, sent = call(halves_body, [half, half], core, whole, rim_tokens)
    other_half = swapped(sent)
    slab, other_half = lax.optimization_barrier((slab, other_half))
    k_rows, state = call(state_body, [struct((blocks, ROWS, POS), BF), struct((lines, 40, POS), BF)], slab)
    states = exchange(state, "ctx_0")
    before, mixed_own, q_rows = call(
        local_body,
        [
            struct((blocks, 32, ROWS), F32), struct((blocks, 32, POS), F32), struct((blocks, ROWS, POS), BF),
        ],
        slab, k_rows,
        flops=2 * blocks * POS * POS * 48,
    )
    mixed, prior, norm = call(
        mix_body,
        [struct((blocks, 32, POS), F32), struct((blocks, 32, ROWS), BF), struct((blocks, 2 * blocks, POS), BF)],
        place, states, before, slab, mixed_own, q_rows,
    )
    norms = exchange(norm, SLAB)
    att_rows, d_mixed, grad_state = call(
        norm_body,
        [struct((blocks, 32, POS), BF), struct((blocks, 32, POS), BF), struct((lines, 40, POS), BF)],
        norms, slab, mixed, q_rows,
    )
    grad_states = exchange(grad_state, "ctx_0")
    after, d_qk, d_val = call(
        back_body,
        [struct((blocks, 32, ROWS), F32), struct((blocks, 32, POS), F32), struct((blocks, 32, POS), F32)],
        slab, d_mixed, prior, q_rows,
        flops=2 * blocks * POS * POS * 144,
    )
    (parts,) = call(
        later_body,
        [struct((blocks, 128, POS), BF)],
        place, grad_states, after, slab, k_rows, d_qk, d_val, att_rows,
    )
    home = exchange(parts, SLAB)
    (grad_parts,) = call(
        grad_body,
        [struct((chips, 8, 128), BF)],
        core, home, own_half, other_half, taps,
        flops=2 * POS * depth * 2 * F,
    )
    arrived = exchange(grad_parts, CHIPS)
    home, _ = lax.optimization_barrier((home, grad_parts))
    attended, g_val, head = call(
        return_body, [struct((POS, E), BF), struct((POS, E), F32), struct((8, E), F32)], home, conv_v
    )
    next_rows = to_next(head, CTX, -1)
    (grad_v,) = call(rim_body, [struct((POS, E), BF)], g_val, next_rows, conv_v)
    scale = float(POS * peers) ** (-0.5)
    (grad_w,) = call(lambda a, b: sum_body(a, b, scale=scale), [struct((2 * F, 2 * F), F32)], arrived)
    return (attended[None], grad_v[None], grad_w)


def solution(mesh):
    split = Mesh(
        mesh.devices.reshape(8, 4, 2, mesh.shape["fsdp"], mesh.shape["batch"]),
        ("ctx_0", "ctx_1", "ctx_2", "fsdp", "batch"),
    )
    in_specs = (
        P("batch", CTX, None),
        P("batch", CTX, "fsdp"),
        P("fsdp", None),
        P(None, "fsdp"),
        P(None, "fsdp"),
        P("batch", CTX, "fsdp"),
    )
    out_specs = (P("batch", CTX, "fsdp"), P("batch", CTX, "fsdp"), P(CTX_BATCH, "fsdp"))
    return jax.shard_map(
        shards, mesh=split, in_specs=in_specs, out_specs=out_specs, check_vma=False
    )
```

```python
import jax
import jax.numpy as jnp
from jax import lax
from jax.experimental import pallas as pl
from jax.experimental.pallas import tpu as pltpu
from jax.sharding import Mesh
from jax.sharding import PartitionSpec as P

F = 16
E = 256
CONV = 3
POS = 128
ROWS = 160
SLAB = ("ctx_1", "ctx_2")
CTX = ("ctx_0", "ctx_1", "ctx_2")
CHIPS = ("ctx_0", "ctx_1", "batch")
CTX_BATCH = ("ctx_0", "ctx_1", "ctx_2", "batch")
BF = jnp.bfloat16
F32 = jnp.float32
eps_norm = 1e-05


def nn(a, b):
    return lax.dot_general(a, b, (((1,), (0,)), ((), ())), preferred_element_type=F32)


def nt(a, b):
    return lax.dot_general(a, b, (((1,), (1,)), ((), ())), preferred_element_type=F32)


def tn(a, b):
    return lax.dot_general(a, b, (((0,), (0,)), ((), ())), preferred_element_type=F32)


def call(body, outs, *args, flops=0, sent=False, scratch=()):
    moved = sum(a.size * a.dtype.itemsize for a in (*args, *outs))
    return pl.pallas_call(
        body,
        out_shape=outs,
        in_specs=[
            pl.BlockSpec(memory_space=pltpu.SMEM if a.dtype == jnp.int32 else pltpu.VMEM) for a in args
        ],
        out_specs=[pl.BlockSpec(memory_space=pl.ANY if sent else pltpu.VMEM)] * len(outs),
        scratch_shapes=scratch,
        cost_estimate=pl.CostEstimate(flops=flops, bytes_accessed=moved, transcendentals=0),
        compiler_params=pltpu.CompilerParams(vmem_limit_bytes=8 << 20),
    )(*args)


def struct(shape, dtype):
    return jax.ShapeDtypeStruct(shape, dtype)


def shifted(w, s):
    return w if s % F == 0 else jnp.concatenate([w[s % F :], w[: s % F]], axis=0)


def rows_of(w):
    parts = [w]
    for s in range(8):
        parts.append(w * shifted(w, s))
    parts.append(w[:8] * w[8:])
    at = lax.broadcasted_iota(jnp.int32, (8, w.shape[1]), 0)
    parts.append(jnp.where(at == 0, 1.0, 0.0).astype(F32))
    return jnp.concatenate(parts, axis=0)


def gains():
    at = lax.broadcasted_iota(jnp.int32, (1, ROWS), 1)
    quad = jnp.where(at < 2 * F, 1.0 / 32.0, 1.0 / 16.0)
    return jnp.where(at < F, 0.25, jnp.where(at < 152, quad, 1.0)).astype(F32)


def eye(size):
    row = lax.broadcasted_iota(jnp.int32, (size, size), 0)
    col = lax.broadcasted_iota(jnp.int32, (size, size), 1)
    return jnp.where(row == col, 1.0, 0.0).astype(BF)


def rows_back(w, y):
    total = 0.25 * y[:F] + (1.0 / 16.0) * w * y[F : 2 * F]
    for s in range(1, 8):
        y_s = y[F * (s + 1) : F * (s + 2)]
        total = total + (1.0 / 16.0) * (
            shifted(w, s) * y_s + shifted(w, F - s) * shifted(y_s, F - s)
        )
    y_8 = y[144:152]
    half = jnp.concatenate([w[8:] * y_8, w[:8] * y_8], axis=0)
    return total + (1.0 / 16.0) * half


def turn_body(w_hbm, cqk_hbm, tok_hbm, val_hbm, grad_hbm, cv_hbm, out_hbm, rim_ref, val_ref, grad_ref, w_buf, cqk_buf, val_buf, out_buf, sems):
    depth = tok_hbm.shape[1]
    half = w_hbm.shape[0] // 2
    pairs = (
        (w_hbm.at[:half], w_buf.at[:half]),
        (w_hbm.at[half:], w_buf.at[half:]),
        (cqk_hbm, cqk_buf),
        (tok_hbm.at[POS - 8 :], rim_ref.at[:, :depth]),
        (val_hbm.at[POS - 8 :], rim_ref.at[:, depth:]),
        (val_hbm, val_buf),
        (grad_hbm, grad_ref),
        (cv_hbm, val_ref.at[POS : POS + CONV]),
    )
    copies = [pltpu.make_async_copy(source, target, sems.at[k]) for k, (source, target) in enumerate(pairs)]
    for copy in copies:
        copy.start()
    square = eye(w_buf.shape[1])
    sent = []
    for k in range(2):
        at = slice(half * k, half * k + half)
        copies[k].wait()
        turned = nt(square, w_buf[at]).astype(BF)
        for part in range(out_buf.shape[0]):
            out_buf[part, :, at] = turned[32 * part : 32 * part + 32]
        sent.append(pltpu.make_async_copy(out_buf.at[:, :, at], out_hbm.at[:, :, at], sems.at[8 + k]))
        sent[-1].start()
    copies[2].wait()
    width = cqk_buf.shape[1]
    row = lax.broadcasted_iota(jnp.int32, (width, width), 0)
    col = lax.broadcasted_iota(jnp.int32, (width, width), 1)
    for tap in range(CONV):
        spread = jnp.where(row == col, jnp.broadcast_to(cqk_buf[tap : tap + 1], (width, width)), 0.0)
        at = POS + 8 + width * tap
        val_ref[at : at + width, :POS] = jnp.broadcast_to(jnp.sum(spread, axis=1, keepdims=True), (width, POS))
    for copy in copies[3:] + sent:
        copy.wait()
    val_ref[:POS] = val_buf[...].astype(F32)


def values_body(val_ref, hval_ref, grad_ref, out_ref, taps_ref):
    for tap in range(CONV):
        at = POS + 8 + 2 * F * tap
        taps_ref[tap] = val_ref[at : at + 2 * F, :POS]
    v0 = val_ref[:POS]
    first, second, third = (val_ref[POS + k : POS + k + 1] for k in range(CONV))
    hv = hval_ref[...].astype(F32)
    at = lax.broadcasted_iota(jnp.int32, v0.shape, 0)
    last, before = (jnp.broadcast_to(hv[k : k + 1], v0.shape) for k in (7, 6))
    v1 = jnp.where(at == 0, last, pltpu.roll(v0, 1, 0))
    v2 = jnp.where(at == 0, before, jnp.where(at == 1, last, pltpu.roll(v0, 2, 0)))
    valued = (first * v0 + second * v1 + third * v2).astype(BF)
    square = eye(E)
    out_ref[0] = nt(square, valued).astype(BF)
    out_ref[1] = nt(square, grad_ref[...]).astype(BF)


def spread_body(w_ref, tok_ref, htok_ref, turned_ref, cqk_ref, out_hbm, conv_buf, sems):
    peers = range(out_hbm.shape[0])
    copies = [
        pltpu.make_async_copy(
            turned_ref.at[k, 32 * peer : 32 * peer + 32], out_hbm.at[peer, 32 * k : 32 * k + 32], sems.at[k, peer]
        )
        for k in range(2)
        for peer in peers
    ]
    for copy in copies:
        copy.start()
    parts, _, deep = w_ref.shape
    own = jnp.zeros((2 * F, POS), F32)
    rim = jnp.zeros((2 * F, htok_ref.shape[0]), F32)
    for part in range(parts):
        w = w_ref[part]
        own = own + nt(w, tok_ref[:, deep * part : deep * part + deep])
        rim = rim + nt(w, htok_ref[:, deep * part : deep * part + deep])
    x0 = own.astype(BF).astype(F32)
    h = rim.astype(BF).astype(F32)
    lane = lax.broadcasted_iota(jnp.int32, x0.shape, 1)
    last, before = (jnp.broadcast_to(h[:, k : k + 1], x0.shape) for k in (7, 6))
    x1 = jnp.where(lane == 0, last, pltpu.roll(x0, 1, 1))
    x2 = jnp.where(lane == 0, before, jnp.where(lane == 1, last, pltpu.roll(x0, 2, 1)))
    conv_buf[...] = (cqk_ref[0] * x0 + cqk_ref[1] * x1 + cqk_ref[2] * x2).astype(BF)
    last = [pltpu.make_async_copy(conv_buf, out_hbm.at[peer, 64:], sems.at[2, peer]) for peer in peers]
    for copy in last:
        copy.start()
    for copy in copies + last:
        copy.wait()


def pack(total):
    side = [total[8 * i : 8 * i + 8, POS:] for i in range(4)]
    return jnp.concatenate([total[:, :POS], jnp.concatenate(side, axis=1)], axis=0)


def unpack(packed):
    side = jnp.concatenate([packed[32:, 32 * i : 32 * i + 32] for i in range(4)], axis=0)
    return jnp.concatenate([packed[:32], side], axis=1)


def state_body(in_ref, krows_ref, out_ref):
    blocks = range(in_ref.shape[0])
    for b in blocks:
        krows_ref[b] = rows_of(in_ref[b, 80:].astype(F32)).astype(BF)
    values = jnp.concatenate([in_ref[b, :32] for b in blocks], axis=1)
    total = pack(nt(values, jnp.concatenate([krows_ref[b] for b in blocks], axis=1))).astype(BF)
    for peer in range(out_ref.shape[0]):
        out_ref[peer] = total


def scores(in_ref, b):
    row = lax.broadcasted_iota(jnp.int32, (POS, POS), 0)
    col = lax.broadcasted_iota(jnp.int32, (POS, POS), 1)
    dotted = tn(in_ref[b, 80:], in_ref[b, 64:80]) * 0.25
    causal = row <= col
    return dotted, causal, jnp.where(causal, 1.0 + dotted + 0.5 * dotted * dotted, 0.0).astype(BF)


def local_body(in_ref, krows_ref, before_ref, mixed_ref, qrows_ref):
    total = jnp.zeros((32, ROWS), F32)
    for b in range(in_ref.shape[0]):
        before_ref[b] = total
        total = total + nt(in_ref[b, :32], krows_ref[b])
        mixed_ref[b] = nn(in_ref[b, :32], scores(in_ref, b)[2])
        qrows_ref[b] = rows_of(in_ref[b, 64:80].astype(F32)).astype(BF)


def mix_body(at_ref, sums_ref, before_ref, in_ref, local_ref, qrows_ref, mixed_ref, prior_ref, out_ref):
    at = at_ref[0]
    total = jnp.zeros(sums_ref.shape[1:], F32)
    for x in range(sums_ref.shape[0]):
        total = total + jnp.where(x < at, sums_ref[x].astype(F32), 0.0)
    total = unpack(total)
    gain = gains()
    squares, products = [], []
    for b in range(in_ref.shape[0]):
        prior = before_ref[b] + total
        prior_ref[b] = prior.astype(BF)
        mixed = local_ref[b] + nn((prior * gain).astype(BF), qrows_ref[b])
        mixed_ref[b] = mixed
        squares.append(jnp.sum(mixed * mixed, axis=0, keepdims=True))
        products.append(jnp.sum(in_ref[b, 32:64].astype(F32) * mixed, axis=0, keepdims=True))
    rows = jnp.concatenate(squares + products, axis=0).astype(BF)
    for peer in range(out_ref.shape[0]):
        out_ref[peer] = rows


def norm_body(sums_ref, in_ref, mixed_ref, qrows_ref, att_ref, dmix_ref, out_ref):
    rows = sums_ref[0].astype(F32)
    for peer in range(1, sums_ref.shape[0]):
        rows = rows + sums_ref[peer].astype(F32)
    rows = rows * (1.0 / E)
    blocks = in_ref.shape[0]
    for b in range(blocks):
        inv = lax.rsqrt(rows[b : b + 1] + eps_norm)
        normed = mixed_ref[b] * inv
        att_ref[b] = normed.astype(BF)
        grad = in_ref[b, 32:64].astype(F32)
        d_mixed = inv * (grad - normed * (inv * rows[blocks + b : blocks + b + 1]))
        dmix_ref[b] = d_mixed.astype(BF)
    d_all = jnp.concatenate([dmix_ref[b] for b in range(blocks)], axis=1)
    total = pack(nt(d_all, jnp.concatenate([qrows_ref[b] for b in range(blocks)], axis=1))).astype(BF)
    for peer in range(out_ref.shape[0]):
        out_ref[peer] = total


def back_body(in_ref, dmix_ref, prior_ref, qrows_ref, after_ref, dqk_ref, dval_ref):
    total = jnp.zeros((32, ROWS), F32)
    for b in reversed(range(in_ref.shape[0])):
        after_ref[b] = total
        total = total + nt(dmix_ref[b], qrows_ref[b])
        queries, keys = in_ref[b, 64:80], in_ref[b, 80:]
        d_mixed = dmix_ref[b]
        dotted, causal, kernel = scores(in_ref, b)
        slope = jnp.where(causal, (1.0 + dotted) * 0.25, 0.0)
        d_score = (tn(in_ref[b, :32], d_mixed) * slope).astype(BF)
        dqk_ref[b, :F] = nn(keys, d_score) + rows_back(queries.astype(F32), tn(prior_ref[b], d_mixed))
        dqk_ref[b, F:] = nt(queries, d_score)
        dval_ref[b] = nt(d_mixed, kernel)


def later_body(at_ref, sums_ref, after_ref, in_ref, krows_ref, dqk_ref, dval_ref, att_ref, out_ref):
    at = at_ref[0]
    total = jnp.zeros(sums_ref.shape[1:], F32)
    for x in range(sums_ref.shape[0]):
        total = total + jnp.where(x > at, sums_ref[x].astype(F32), 0.0)
    total = unpack(total)
    gain = gains()
    for b in range(in_ref.shape[0]):
        later = after_ref[b] + total
        keys = in_ref[b, 80:].astype(F32)
        d_key = dqk_ref[b, F:] + rows_back(keys, tn(later.astype(BF), in_ref[b, :32]))
        part = jnp.concatenate([dqk_ref[b, :F], d_key], axis=0).astype(BF)
        first, at_row = b - b % 2, 32 * (b % 2)
        out_ref[first, at_row : at_row + 32] = part
        out_ref[first + 1, at_row : at_row + 32] = part
        out_ref[b, 64:96] = att_ref[b]
        out_ref[b, 96:] = (dval_ref[b] + nn((later * gain).astype(BF), krows_ref[b])).astype(BF)


def halves_body(core_ref, tok_ref, htok_ref, mine_ref, theirs_ref):
    for refs, wanted in (((mine_ref, theirs_ref), 0), ((theirs_ref, mine_ref), 1)):

        @pl.when(core_ref[0] == wanted)
        def _(refs=refs):
            for in_ref, at in ((tok_ref, slice(0, POS)), (htok_ref, slice(POS, POS + 8))):
                for m in range(in_ref.shape[1] // 256):
                    left = in_ref[:, 256 * m : 256 * m + 128]
                    right = in_ref[:, 256 * m + 128 : 256 * m + 256]
                    cols = slice(128 * m, 128 * m + 128)
                    refs[0][at, cols] = jnp.concatenate([left[:, :64], right[:, :64]], axis=1)
                    refs[1][at, cols] = jnp.concatenate([left[:, 64:], right[:, 64:]], axis=1)


def grad_body(core_ref, sums_ref, tok_ref, other_ref, cqk_ref, out_hbm, out_ref, sems):
    pair = sums_ref[0, : 4 * F].astype(F32)
    for peer in range(1, sums_ref.shape[0]):
        pair = pair + sums_ref[peer, : 4 * F].astype(F32)
    first, second = pair[: 2 * F], pair[2 * F :]
    core = core_ref[0]
    lane = lax.broadcasted_iota(jnp.int32, first.shape, 1)

    def ahead(d, nxt, by):
        return jnp.where(lane < POS - by, pltpu.roll(d, POS - by, 1), pltpu.roll(nxt, POS - by, 1))

    zero = jnp.zeros_like(first)
    of_first = cqk_ref[0] * first + cqk_ref[1] * ahead(first, second, 1) + cqk_ref[2] * ahead(first, second, 2)
    of_second = cqk_ref[0] * second + cqk_ref[1] * ahead(second, zero, 1) + cqk_ref[2] * ahead(second, zero, 2)
    to_last = pltpu.roll(cqk_ref[2] * first, 6, 1)
    near = pltpu.roll(cqk_ref[1] * first, 7, 1) + to_last
    rim = jnp.where(lane == 6, to_last, jnp.where(lane == 7, near, 0.0))[:, :8]
    own_b = jnp.where(core == 0, of_first, of_second).astype(BF)
    other_b = jnp.where(core == 0, of_second, of_first).astype(BF)
    rim_own = jnp.where(core == 0, rim, 0.0).astype(BF)
    rim_other = jnp.where(core == 0, 0.0, rim).astype(BF)

    group = lax.broadcasted_iota(jnp.int32, (8, 128), 1) // 32
    chunk = 512
    copies = []
    for start in range(0, tok_ref.shape[1], chunk):
        at = slice(start, start + chunk)
        part = nn(own_b, tok_ref[:POS, at]) + nn(other_b, other_ref[:POS, at])
        part = part + nn(rim_own, tok_ref[POS:, at]) + nn(rim_other, other_ref[POS:, at])
        for at_lane in range(0, chunk, 128):
            blocks = [part[8 * i : 8 * i + 8, at_lane : at_lane + 128] for i in range(4)]
            for q in range(4):
                moved = [pltpu.roll(b, 32 * ((i - q) % 4), 1) if i != q else b for i, b in enumerate(blocks)]
                packed = jnp.where(
                    group == 0, moved[0], jnp.where(group == 1, moved[1], jnp.where(group == 2, moved[2], moved[3]))
                )
                out_ref[(start + at_lane) // 32 + q] = packed.astype(out_ref.dtype)
        tiles = slice(start // 32, (start + chunk) // 32)
        copies.append(pltpu.make_async_copy(out_ref.at[tiles], out_hbm.at[tiles], sems.at[start // chunk]))
        copies[-1].start()
    for copy in copies:
        copy.wait()


def return_body(in_ref, cv_ref, att_ref, gval_ref, head_ref):
    square = eye(POS)
    peers = range(in_ref.shape[0])
    att = jnp.concatenate([in_ref[j, 64:96] for j in peers], axis=0)
    d_rows = jnp.concatenate([in_ref[j, 96:] for j in peers], axis=0)
    att_ref[...] = nt(square, att).astype(BF)
    dv = nt(square, d_rows)
    head_ref[...] = dv[:8]
    at = lax.broadcasted_iota(jnp.int32, dv.shape, 0)
    gval = cv_ref[0:1] * dv
    gval = gval + cv_ref[1:2] * jnp.where(at < POS - 1, pltpu.roll(dv, POS - 1, 0), 0.0)
    gval = gval + cv_ref[2:3] * jnp.where(at < POS - 2, pltpu.roll(dv, POS - 2, 0), 0.0)
    gval_ref[...] = gval


def rim_body(gval_ref, next_ref, cv_ref, out_ref):
    out_ref[...] = gval_ref[...].astype(BF)
    nxt = next_ref[...]
    at = lax.broadcasted_iota(jnp.int32, nxt.shape, 0)
    c1, c2 = cv_ref[1:2], cv_ref[2:3]
    first, second = (jnp.broadcast_to(nxt[k : k + 1], nxt.shape) for k in (0, 1))
    more = jnp.where(at == 6, c2 * first, jnp.where(at == 7, c1 * first + c2 * second, 0.0))
    out_ref[POS - 8 :] = (gval_ref[POS - 8 :] + more).astype(BF)


def sum_body(parts_ref, out_ref, *, scale):
    totals = [parts_ref[k].astype(F32) for k in range(8)]
    for k in range(8, parts_ref.shape[0]):
        totals[k % 8] = totals[k % 8] + parts_ref[k].astype(F32)
    while len(totals) > 1:
        totals = [a + b for a, b in zip(totals[::2], totals[1::2])]
    total = totals[0] * scale
    stacked = jnp.concatenate([total] + [pltpu.roll(total, 128 - 32 * i, 1) for i in (1, 2, 3)], axis=0)
    square = jnp.concatenate([stacked, jnp.zeros((96, 128), F32)], axis=0).T
    out_ref[...] = square[:32, :32]


def to_next(value, axes, by):
    size = lax.axis_size(axes)
    pairs = [(i, i + by) for i in range(size) if 0 <= i + by < size]
    return lax.ppermute(value, axes, pairs)


def swapped(value):
    return lax.ppermute(value, "ctx_2", [(0, 1), (1, 0)])


def exchange(value, axes):
    return lax.all_to_all(value, axes, split_axis=0, concat_axis=0, tiled=True)


def shards(inputs, values, w_qk, conv_qk, conv_v, d_attn):
    tokens, own_values = inputs[0], values[0]
    depth = tokens.shape[1]
    splits = lax.axis_size("fsdp")
    lines = lax.axis_size("ctx_0")
    blocks = lax.axis_size(SLAB)
    peers = lax.axis_size(CTX_BATCH)
    deep = w_qk.shape[0]
    chips = lax.axis_size(CHIPS)
    place = lax.axis_index("ctx_0").astype(jnp.int32).reshape(1)
    core = lax.axis_index("ctx_2").astype(jnp.int32).reshape(1)

    sources = (w_qk, conv_qk, tokens, own_values, d_attn[0], conv_v)
    fetched = [
        struct((splits, 2 * F, deep), BF), struct((8, depth + E), BF),
        struct((POS + 8 + CONV * 2 * F, E), F32), struct((POS, E), BF),
    ]
    turned, rim, own_values, own_grad = pl.pallas_call(
        turn_body,
        out_shape=fetched,
        in_specs=[pl.BlockSpec(memory_space=pltpu.HBM)] * len(sources),
        out_specs=[pl.BlockSpec(memory_space=pl.ANY)] + [pl.BlockSpec(memory_space=pltpu.VMEM)] * (len(fetched) - 1),
        scratch_shapes=[
            pltpu.VMEM(w_qk.shape, BF), pltpu.VMEM(conv_qk.shape, F32), pltpu.VMEM((POS, E), BF),
            pltpu.VMEM((splits, 2 * F, deep), BF), pltpu.SemaphoreType.DMA((10,)),
        ],
        compiler_params=pltpu.CompilerParams(vmem_limit_bytes=60 * 1024 * 1024),
        name="turn",
    )(*sources)
    weights = exchange(turned, "fsdp")
    rim = to_next(rim, CTX, 1)
    rim_tokens, rim_values = rim[:, :depth], rim[:, depth:]

    value_rows, taps = call(
        values_body,
        [struct((2, E, POS), BF), struct((CONV, 2 * F, POS), F32)],
        own_values, rim_values, own_grad,
    )
    (spread,) = call(
        spread_body, [struct((blocks, 96, POS), BF)], weights, tokens, rim_tokens, value_rows, taps,
        sent=True,
        scratch=[pltpu.VMEM((2 * F, POS), BF), pltpu.SemaphoreType.DMA((3, blocks))],
    )
    whole, rim_tokens, spread = lax.optimization_barrier((tokens, rim_tokens, spread))
    slab = exchange(spread, SLAB)
    half = struct((POS + 8, depth // 2), BF)
    own_half, sent = call(halves_body, [half, half], core, whole, rim_tokens)
    other_half = swapped(sent)
    slab, other_half = lax.optimization_barrier((slab, other_half))
    k_rows, state = call(state_body, [struct((blocks, ROWS, POS), BF), struct((lines, 40, POS), BF)], slab)
    states = exchange(state, "ctx_0")
    before, mixed_own, q_rows = call(
        local_body,
        [
            struct((blocks, 32, ROWS), F32), struct((blocks, 32, POS), F32), struct((blocks, ROWS, POS), BF),
        ],
        slab, k_rows,
        flops=2 * blocks * POS * POS * 48,
    )
    mixed, prior, norm = call(
        mix_body,
        [struct((blocks, 32, POS), F32), struct((blocks, 32, ROWS), BF), struct((blocks, 2 * blocks, POS), BF)],
        place, states, before, slab, mixed_own, q_rows,
    )
    norms = exchange(norm, SLAB)
    att_rows, d_mixed, grad_state = call(
        norm_body,
        [struct((blocks, 32, POS), BF), struct((blocks, 32, POS), BF), struct((lines, 40, POS), BF)],
        norms, slab, mixed, q_rows,
    )
    grad_states = exchange(grad_state, "ctx_0")
    after, d_qk, d_val = call(
        back_body,
        [struct((blocks, 32, ROWS), F32), struct((blocks, 32, POS), F32), struct((blocks, 32, POS), F32)],
        slab, d_mixed, prior, q_rows,
        flops=2 * blocks * POS * POS * 144,
    )
    (parts,) = call(
        later_body,
        [struct((blocks, 128, POS), BF)],
        place, grad_states, after, slab, k_rows, d_qk, d_val, att_rows,
    )
    home = exchange(parts, SLAB)
    (grad_parts,) = call(
        grad_body,
        [struct((chips, 8, 128), BF)],
        core, home, own_half, other_half, taps,
        flops=2 * POS * depth * 2 * F, sent=True,
        scratch=[pltpu.VMEM((chips, 8, 128), BF), pltpu.SemaphoreType.DMA((depth // 1024,))],
    )
    arrived = exchange(grad_parts, CHIPS)
    home, _ = lax.optimization_barrier((home, grad_parts))
    attended, g_val, head = call(
        return_body, [struct((POS, E), BF), struct((POS, E), F32), struct((8, E), F32)], home, conv_v
    )
    next_rows = to_next(head, CTX, -1)
    (grad_v,) = call(rim_body, [struct((POS, E), BF)], g_val, next_rows, conv_v)
    scale = float(POS * peers) ** (-0.5)
    (grad_w,) = call(lambda a, b: sum_body(a, b, scale=scale), [struct((2 * F, 2 * F), F32)], arrived)
    return (attended[None], grad_v[None], grad_w)


def solution(mesh):
    split = Mesh(
        mesh.devices.reshape(8, 4, 2, mesh.shape["fsdp"], mesh.shape["batch"]),
        ("ctx_0", "ctx_1", "ctx_2", "fsdp", "batch"),
    )
    in_specs = (
        P("batch", CTX, None),
        P("batch", CTX, "fsdp"),
        P("fsdp", None),
        P(None, "fsdp"),
        P(None, "fsdp"),
        P("batch", CTX, "fsdp"),
    )
    out_specs = (P("batch", CTX, "fsdp"), P("batch", CTX, "fsdp"), P(CTX_BATCH, "fsdp"))
    return jax.shard_map(
        shards, mesh=split, in_specs=in_specs, out_specs=out_specs, check_vma=False
    )
```

```python
import jax
import jax.numpy as jnp
from jax import lax
from jax.experimental import pallas as pl
from jax.experimental.pallas import tpu as pltpu
from jax.sharding import Mesh
from jax.sharding import PartitionSpec as P

F = 16
E = 256
CONV = 3
POS = 128
ROWS = 160
SLAB = ("ctx_1", "ctx_2")
CTX = ("ctx_0", "ctx_1", "ctx_2")
CHIPS = ("ctx_0", "ctx_1", "batch")
CTX_BATCH = ("ctx_0", "ctx_1", "ctx_2", "batch")
BF = jnp.bfloat16
F32 = jnp.float32
eps_norm = 1e-05


def nn(a, b):
    return lax.dot_general(a, b, (((1,), (0,)), ((), ())), preferred_element_type=F32)


def nt(a, b):
    return lax.dot_general(a, b, (((1,), (1,)), ((), ())), preferred_element_type=F32)


def tn(a, b):
    return lax.dot_general(a, b, (((0,), (0,)), ((), ())), preferred_element_type=F32)


def call(body, outs, *args, flops=0):
    moved = sum(a.size * a.dtype.itemsize for a in (*args, *outs))
    return pl.pallas_call(
        body,
        out_shape=outs,
        in_specs=[
            pl.BlockSpec(memory_space=pltpu.SMEM if a.dtype == jnp.int32 else pltpu.VMEM) for a in args
        ],
        out_specs=[pl.BlockSpec(memory_space=pltpu.VMEM)] * len(outs),
        cost_estimate=pl.CostEstimate(flops=flops, bytes_accessed=moved, transcendentals=0),
        compiler_params=pltpu.CompilerParams(vmem_limit_bytes=8 << 20),
    )(*args)


def struct(shape, dtype):
    return jax.ShapeDtypeStruct(shape, dtype)


def shifted(w, s):
    return w if s % F == 0 else jnp.concatenate([w[s % F :], w[: s % F]], axis=0)


def rows_of(w):
    parts = [w]
    for s in range(8):
        parts.append(w * shifted(w, s))
    parts.append(w[:8] * w[8:])
    at = lax.broadcasted_iota(jnp.int32, (8, w.shape[1]), 0)
    parts.append(jnp.where(at == 0, 1.0, 0.0).astype(F32))
    return jnp.concatenate(parts, axis=0)


def gains():
    at = lax.broadcasted_iota(jnp.int32, (1, ROWS), 1)
    quad = jnp.where(at < 2 * F, 1.0 / 32.0, 1.0 / 16.0)
    return jnp.where(at < F, 0.25, jnp.where(at < 152, quad, 1.0)).astype(F32)


def eye(size):
    row = lax.broadcasted_iota(jnp.int32, (size, size), 0)
    col = lax.broadcasted_iota(jnp.int32, (size, size), 1)
    return jnp.where(row == col, 1.0, 0.0).astype(BF)


def rows_back(w, y):
    total = 0.25 * y[:F] + (1.0 / 16.0) * w * y[F : 2 * F]
    for s in range(1, 8):
        y_s = y[F * (s + 1) : F * (s + 2)]
        total = total + (1.0 / 16.0) * (
            shifted(w, s) * y_s + shifted(w, F - s) * shifted(y_s, F - s)
        )
    y_8 = y[144:152]
    half = jnp.concatenate([w[8:] * y_8, w[:8] * y_8], axis=0)
    return total + (1.0 / 16.0) * half


def turn_body(w_hbm, cqk_hbm, tok_hbm, val_hbm, grad_hbm, cv_hbm, out_ref, rim_ref, val_ref, grad_ref, w_buf, cqk_buf, val_buf, sems):
    depth = tok_hbm.shape[1]
    pairs = (
        (w_hbm, w_buf),
        (cqk_hbm, cqk_buf),
        (tok_hbm.at[POS - 8 :], rim_ref.at[:, :depth]),
        (val_hbm.at[POS - 8 :], rim_ref.at[:, depth:]),
        (val_hbm, val_buf),
        (grad_hbm, grad_ref),
        (cv_hbm, val_ref.at[POS : POS + CONV]),
    )
    copies = [pltpu.make_async_copy(source, target, sems.at[k]) for k, (source, target) in enumerate(pairs)]
    for copy in copies:
        copy.start()
    copies[0].wait()
    turned = nt(eye(w_buf.shape[1]), w_buf[...]).astype(BF)
    for part in range(out_ref.shape[0]):
        out_ref[part] = turned[32 * part : 32 * part + 32]
    copies[1].wait()
    width = cqk_buf.shape[1]
    row = lax.broadcasted_iota(jnp.int32, (width, width), 0)
    col = lax.broadcasted_iota(jnp.int32, (width, width), 1)
    for tap in range(CONV):
        spread = jnp.where(row == col, jnp.broadcast_to(cqk_buf[tap : tap + 1], (width, width)), 0.0)
        at = POS + 8 + width * tap
        val_ref[at : at + width, :POS] = jnp.broadcast_to(jnp.sum(spread, axis=1, keepdims=True), (width, POS))
    for copy in copies[2:]:
        copy.wait()
    val_ref[:POS] = val_buf[...].astype(F32)


def values_body(val_ref, hval_ref, grad_ref, out_ref, taps_ref):
    for tap in range(CONV):
        at = POS + 8 + 2 * F * tap
        taps_ref[tap] = val_ref[at : at + 2 * F, :POS]
    v0 = val_ref[:POS]
    first, second, third = (val_ref[POS + k : POS + k + 1] for k in range(CONV))
    hv = hval_ref[...].astype(F32)
    at = lax.broadcasted_iota(jnp.int32, v0.shape, 0)
    last, before = (jnp.broadcast_to(hv[k : k + 1], v0.shape) for k in (7, 6))
    v1 = jnp.where(at == 0, last, pltpu.roll(v0, 1, 0))
    v2 = jnp.where(at == 0, before, jnp.where(at == 1, last, pltpu.roll(v0, 2, 0)))
    valued = (first * v0 + second * v1 + third * v2).astype(BF)
    square = eye(E)
    out_ref[0] = nt(square, valued).astype(BF)
    out_ref[1] = nt(square, grad_ref[...]).astype(BF)


def spread_body(w_ref, tok_ref, htok_ref, turned_ref, cqk_ref, out_ref):
    parts, _, deep = w_ref.shape
    own = jnp.zeros((2 * F, POS), F32)
    rim = jnp.zeros((2 * F, htok_ref.shape[0]), F32)
    for part in range(parts):
        w = w_ref[part]
        own = own + nt(w, tok_ref[:, deep * part : deep * part + deep])
        rim = rim + nt(w, htok_ref[:, deep * part : deep * part + deep])
    x0 = own.astype(BF).astype(F32)
    h = rim.astype(BF).astype(F32)
    lane = lax.broadcasted_iota(jnp.int32, x0.shape, 1)
    last, before = (jnp.broadcast_to(h[:, k : k + 1], x0.shape) for k in (7, 6))
    x1 = jnp.where(lane == 0, last, pltpu.roll(x0, 1, 1))
    x2 = jnp.where(lane == 0, before, jnp.where(lane == 1, last, pltpu.roll(x0, 2, 1)))
    conv = (cqk_ref[0] * x0 + cqk_ref[1] * x1 + cqk_ref[2] * x2).astype(BF)
    for peer in range(out_ref.shape[0]):
        out_ref[peer, :32] = turned_ref[0, 32 * peer : 32 * peer + 32]
        out_ref[peer, 32:64] = turned_ref[1, 32 * peer : 32 * peer + 32]
        out_ref[peer, 64:] = conv


def pack(total):
    side = [total[8 * i : 8 * i + 8, POS:] for i in range(4)]
    return jnp.concatenate([total[:, :POS], jnp.concatenate(side, axis=1)], axis=0)


def unpack(packed):
    side = jnp.concatenate([packed[32:, 32 * i : 32 * i + 32] for i in range(4)], axis=0)
    return jnp.concatenate([packed[:32], side], axis=1)


def state_body(in_ref, krows_ref, out_ref):
    blocks = range(in_ref.shape[0])
    for b in blocks:
        krows_ref[b] = rows_of(in_ref[b, 80:].astype(F32)).astype(BF)
    values = jnp.concatenate([in_ref[b, :32] for b in blocks], axis=1)
    total = pack(nt(values, jnp.concatenate([krows_ref[b] for b in blocks], axis=1))).astype(BF)
    for peer in range(out_ref.shape[0]):
        out_ref[peer] = total


def scores(in_ref, b):
    row = lax.broadcasted_iota(jnp.int32, (POS, POS), 0)
    col = lax.broadcasted_iota(jnp.int32, (POS, POS), 1)
    dotted = tn(in_ref[b, 80:], in_ref[b, 64:80]) * 0.25
    causal = row <= col
    return dotted, causal, jnp.where(causal, 1.0 + dotted + 0.5 * dotted * dotted, 0.0).astype(BF)


def local_body(in_ref, krows_ref, before_ref, mixed_ref, qrows_ref):
    total = jnp.zeros((32, ROWS), F32)
    for b in range(in_ref.shape[0]):
        before_ref[b] = total
        total = total + nt(in_ref[b, :32], krows_ref[b])
        mixed_ref[b] = nn(in_ref[b, :32], scores(in_ref, b)[2])
        qrows_ref[b] = rows_of(in_ref[b, 64:80].astype(F32)).astype(BF)


def mix_body(at_ref, sums_ref, before_ref, in_ref, local_ref, qrows_ref, mixed_ref, prior_ref, out_ref):
    at = at_ref[0]
    total = jnp.zeros(sums_ref.shape[1:], F32)
    for x in range(sums_ref.shape[0]):
        total = total + jnp.where(x < at, sums_ref[x].astype(F32), 0.0)
    total = unpack(total)
    gain = gains()
    squares, products = [], []
    for b in range(in_ref.shape[0]):
        prior = before_ref[b] + total
        prior_ref[b] = prior.astype(BF)
        mixed = local_ref[b] + nn((prior * gain).astype(BF), qrows_ref[b])
        mixed_ref[b] = mixed
        squares.append(jnp.sum(mixed * mixed, axis=0, keepdims=True))
        products.append(jnp.sum(in_ref[b, 32:64].astype(F32) * mixed, axis=0, keepdims=True))
    rows = jnp.concatenate(squares + products, axis=0).astype(BF)
    for peer in range(out_ref.shape[0]):
        out_ref[peer] = rows


def norm_body(sums_ref, in_ref, mixed_ref, qrows_ref, att_ref, dmix_ref, out_ref):
    rows = sums_ref[0].astype(F32)
    for peer in range(1, sums_ref.shape[0]):
        rows = rows + sums_ref[peer].astype(F32)
    rows = rows * (1.0 / E)
    blocks = in_ref.shape[0]
    for b in range(blocks):
        inv = lax.rsqrt(rows[b : b + 1] + eps_norm)
        normed = mixed_ref[b] * inv
        att_ref[b] = normed.astype(BF)
        grad = in_ref[b, 32:64].astype(F32)
        d_mixed = inv * (grad - normed * (inv * rows[blocks + b : blocks + b + 1]))
        dmix_ref[b] = d_mixed.astype(BF)
    d_all = jnp.concatenate([dmix_ref[b] for b in range(blocks)], axis=1)
    total = pack(nt(d_all, jnp.concatenate([qrows_ref[b] for b in range(blocks)], axis=1))).astype(BF)
    for peer in range(out_ref.shape[0]):
        out_ref[peer] = total


def back_body(in_ref, dmix_ref, prior_ref, qrows_ref, after_ref, dqk_ref, dval_ref):
    total = jnp.zeros((32, ROWS), F32)
    for b in reversed(range(in_ref.shape[0])):
        after_ref[b] = total
        total = total + nt(dmix_ref[b], qrows_ref[b])
        queries, keys = in_ref[b, 64:80], in_ref[b, 80:]
        d_mixed = dmix_ref[b]
        dotted, causal, kernel = scores(in_ref, b)
        slope = jnp.where(causal, (1.0 + dotted) * 0.25, 0.0)
        d_score = (tn(in_ref[b, :32], d_mixed) * slope).astype(BF)
        dqk_ref[b, :F] = nn(keys, d_score) + rows_back(queries.astype(F32), tn(prior_ref[b], d_mixed))
        dqk_ref[b, F:] = nt(queries, d_score)
        dval_ref[b] = nt(d_mixed, kernel)


def later_body(at_ref, sums_ref, after_ref, in_ref, krows_ref, dqk_ref, dval_ref, att_ref, out_ref):
    at = at_ref[0]
    total = jnp.zeros(sums_ref.shape[1:], F32)
    for x in range(sums_ref.shape[0]):
        total = total + jnp.where(x > at, sums_ref[x].astype(F32), 0.0)
    total = unpack(total)
    gain = gains()
    for b in range(in_ref.shape[0]):
        later = after_ref[b] + total
        keys = in_ref[b, 80:].astype(F32)
        d_key = dqk_ref[b, F:] + rows_back(keys, tn(later.astype(BF), in_ref[b, :32]))
        part = jnp.concatenate([dqk_ref[b, :F], d_key], axis=0).astype(BF)
        first, at_row = b - b % 2, 32 * (b % 2)
        out_ref[first, at_row : at_row + 32] = part
        out_ref[first + 1, at_row : at_row + 32] = part
        out_ref[b, 64:96] = att_ref[b]
        out_ref[b, 96:] = (dval_ref[b] + nn((later * gain).astype(BF), krows_ref[b])).astype(BF)


def halves_body(core_ref, after_ref, tok_ref, htok_ref, mine_ref, theirs_ref):
    for refs, wanted in (((mine_ref, theirs_ref), 0), ((theirs_ref, mine_ref), 1)):

        @pl.when(core_ref[0] == wanted)
        def _(refs=refs):
            for in_ref, at in ((tok_ref, slice(0, POS)), (htok_ref, slice(POS, POS + 8))):
                for m in range(in_ref.shape[1] // 256):
                    left = in_ref[:, 256 * m : 256 * m + 128]
                    right = in_ref[:, 256 * m + 128 : 256 * m + 256]
                    cols = slice(128 * m, 128 * m + 128)
                    refs[0][at, cols] = jnp.concatenate([left[:, :64], right[:, :64]], axis=1)
                    refs[1][at, cols] = jnp.concatenate([left[:, 64:], right[:, 64:]], axis=1)


def grad_body(core_ref, sums_ref, tok_ref, other_ref, cqk_ref, out_ref):
    pair = sums_ref[0, : 4 * F].astype(F32)
    for peer in range(1, sums_ref.shape[0]):
        pair = pair + sums_ref[peer, : 4 * F].astype(F32)
    first, second = pair[: 2 * F], pair[2 * F :]
    core = core_ref[0]
    lane = lax.broadcasted_iota(jnp.int32, first.shape, 1)

    def ahead(d, nxt, by):
        return jnp.where(lane < POS - by, pltpu.roll(d, POS - by, 1), pltpu.roll(nxt, POS - by, 1))

    zero = jnp.zeros_like(first)
    of_first = cqk_ref[0] * first + cqk_ref[1] * ahead(first, second, 1) + cqk_ref[2] * ahead(first, second, 2)
    of_second = cqk_ref[0] * second + cqk_ref[1] * ahead(second, zero, 1) + cqk_ref[2] * ahead(second, zero, 2)
    to_last = pltpu.roll(cqk_ref[2] * first, 6, 1)
    near = pltpu.roll(cqk_ref[1] * first, 7, 1) + to_last
    rim = jnp.where(lane == 6, to_last, jnp.where(lane == 7, near, 0.0))[:, :8]
    own_b = jnp.where(core == 0, of_first, of_second).astype(BF)
    other_b = jnp.where(core == 0, of_second, of_first).astype(BF)
    rim_own = jnp.where(core == 0, rim, 0.0).astype(BF)
    rim_other = jnp.where(core == 0, 0.0, rim).astype(BF)

    group = lax.broadcasted_iota(jnp.int32, (8, 128), 1) // 32
    chunk = 512
    for start in range(0, tok_ref.shape[1], chunk):
        at = slice(start, start + chunk)
        part = nn(own_b, tok_ref[:POS, at]) + nn(other_b, other_ref[:POS, at])
        part = part + nn(rim_own, tok_ref[POS:, at]) + nn(rim_other, other_ref[POS:, at])
        for at_lane in range(0, chunk, 128):
            blocks = [part[8 * i : 8 * i + 8, at_lane : at_lane + 128] for i in range(4)]
            for q in range(4):
                moved = [pltpu.roll(b, 32 * ((i - q) % 4), 1) if i != q else b for i, b in enumerate(blocks)]
                packed = jnp.where(
                    group == 0, moved[0], jnp.where(group == 1, moved[1], jnp.where(group == 2, moved[2], moved[3]))
                )
                out_ref[(start + at_lane) // 32 + q] = packed.astype(out_ref.dtype)


def return_body(in_ref, cv_ref, att_ref, gval_ref, head_ref):
    square = eye(POS)
    peers = range(in_ref.shape[0])
    att = jnp.concatenate([in_ref[j, 64:96] for j in peers], axis=0)
    d_rows = jnp.concatenate([in_ref[j, 96:] for j in peers], axis=0)
    att_ref[...] = nt(square, att).astype(BF)
    dv = nt(square, d_rows)
    head_ref[...] = dv[:8]
    at = lax.broadcasted_iota(jnp.int32, dv.shape, 0)
    gval = cv_ref[0:1] * dv
    gval = gval + cv_ref[1:2] * jnp.where(at < POS - 1, pltpu.roll(dv, POS - 1, 0), 0.0)
    gval = gval + cv_ref[2:3] * jnp.where(at < POS - 2, pltpu.roll(dv, POS - 2, 0), 0.0)
    gval_ref[...] = gval


def rim_body(gval_ref, next_ref, cv_ref, out_ref):
    out_ref[...] = gval_ref[...].astype(BF)
    nxt = next_ref[...]
    at = lax.broadcasted_iota(jnp.int32, nxt.shape, 0)
    c1, c2 = cv_ref[1:2], cv_ref[2:3]
    first, second = (jnp.broadcast_to(nxt[k : k + 1], nxt.shape) for k in (0, 1))
    more = jnp.where(at == 6, c2 * first, jnp.where(at == 7, c1 * first + c2 * second, 0.0))
    out_ref[POS - 8 :] = (gval_ref[POS - 8 :] + more).astype(BF)


def sum_body(parts_ref, out_ref, *, scale):
    totals = [parts_ref[k].astype(F32) for k in range(8)]
    for k in range(8, parts_ref.shape[0]):
        totals[k % 8] = totals[k % 8] + parts_ref[k].astype(F32)
    while len(totals) > 1:
        totals = [a + b for a, b in zip(totals[::2], totals[1::2])]
    total = totals[0] * scale
    stacked = jnp.concatenate([total] + [pltpu.roll(total, 128 - 32 * i, 1) for i in (1, 2, 3)], axis=0)
    square = jnp.concatenate([stacked, jnp.zeros((96, 128), F32)], axis=0).T
    out_ref[...] = square[:32, :32]


def to_next(value, axes, by):
    size = lax.axis_size(axes)
    pairs = [(i, i + by) for i in range(size) if 0 <= i + by < size]
    return lax.ppermute(value, axes, pairs)


def swapped(value):
    return lax.ppermute(value, "ctx_2", [(0, 1), (1, 0)])


def exchange(value, axes):
    return lax.all_to_all(value, axes, split_axis=0, concat_axis=0, tiled=True)


def shards(inputs, values, w_qk, conv_qk, conv_v, d_attn):
    tokens, own_values = inputs[0], values[0]
    depth = tokens.shape[1]
    splits = lax.axis_size("fsdp")
    lines = lax.axis_size("ctx_0")
    blocks = lax.axis_size(SLAB)
    peers = lax.axis_size(CTX_BATCH)
    deep = w_qk.shape[0]
    chips = lax.axis_size(CHIPS)
    place = lax.axis_index("ctx_0").astype(jnp.int32).reshape(1)
    core = lax.axis_index("ctx_2").astype(jnp.int32).reshape(1)
    place, core, w_qk = lax.optimization_barrier((place, core, w_qk))

    sources = (w_qk, conv_qk, tokens, own_values, d_attn[0], conv_v)
    fetched = [
        struct((splits, 2 * F, deep), BF), struct((8, depth + E), BF),
        struct((POS + 8 + CONV * 2 * F, E), F32), struct((POS, E), BF),
    ]
    turned, rim, own_values, own_grad = pl.pallas_call(
        turn_body,
        out_shape=fetched,
        in_specs=[pl.BlockSpec(memory_space=pltpu.HBM)] * len(sources),
        out_specs=[pl.BlockSpec(memory_space=pltpu.VMEM)] * len(fetched),
        scratch_shapes=[
            pltpu.VMEM(w_qk.shape, BF), pltpu.VMEM(conv_qk.shape, F32), pltpu.VMEM((POS, E), BF), pltpu.SemaphoreType.DMA((7,))
        ],
        compiler_params=pltpu.CompilerParams(vmem_limit_bytes=60 * 1024 * 1024),
        name="turn",
    )(*sources)
    weights = exchange(turned, "fsdp")
    rim = to_next(rim, CTX, 1)
    rim_tokens, rim_values = rim[:, :depth], rim[:, depth:]

    value_rows, taps = call(
        values_body,
        [struct((2, E, POS), BF), struct((CONV, 2 * F, POS), F32)],
        own_values, rim_values, own_grad,
    )
    (spread,) = call(spread_body, [struct((blocks, 96, POS), BF)], weights, tokens, rim_tokens, value_rows, taps)
    slab = exchange(spread, SLAB)
    k_rows, state = call(state_body, [struct((blocks, ROWS, POS), BF), struct((lines, 40, POS), BF)], slab)
    states = exchange(state, "ctx_0")
    half = struct((POS + 8, depth // 2), BF)
    own_half, sent = call(halves_body, [half, half], core, k_rows, tokens, rim_tokens)
    other_half = swapped(sent)
    before, mixed_own, q_rows = call(
        local_body,
        [
            struct((blocks, 32, ROWS), F32), struct((blocks, 32, POS), F32), struct((blocks, ROWS, POS), BF),
        ],
        slab, k_rows,
        flops=2 * blocks * POS * POS * 48,
    )
    other_half, mixed_own = lax.optimization_barrier((other_half, mixed_own))
    mixed, prior, norm = call(
        mix_body,
        [struct((blocks, 32, POS), F32), struct((blocks, 32, ROWS), BF), struct((blocks, 2 * blocks, POS), BF)],
        place, states, before, slab, mixed_own, q_rows,
    )
    norms = exchange(norm, SLAB)
    att_rows, d_mixed, grad_state = call(
        norm_body,
        [struct((blocks, 32, POS), BF), struct((blocks, 32, POS), BF), struct((lines, 40, POS), BF)],
        norms, slab, mixed, q_rows,
    )
    grad_states = exchange(grad_state, "ctx_0")
    after, d_qk, d_val = call(
        back_body,
        [struct((blocks, 32, ROWS), F32), struct((blocks, 32, POS), F32), struct((blocks, 32, POS), F32)],
        slab, d_mixed, prior, q_rows,
        flops=2 * blocks * POS * POS * 144,
    )
    (parts,) = call(
        later_body,
        [struct((blocks, 128, POS), BF)],
        place, grad_states, after, slab, k_rows, d_qk, d_val, att_rows,
    )
    home = exchange(parts, SLAB)
    (grad_parts,) = call(
        grad_body,
        [struct((chips, 8, 128), BF)],
        core, home, own_half, other_half, taps,
        flops=2 * POS * depth * 2 * F,
    )
    arrived = exchange(grad_parts, CHIPS)
    home, _ = lax.optimization_barrier((home, grad_parts))
    attended, g_val, head = call(
        return_body, [struct((POS, E), BF), struct((POS, E), F32), struct((8, E), F32)], home, conv_v
    )
    next_rows = to_next(head, CTX, -1)
    (grad_v,) = call(rim_body, [struct((POS, E), BF)], g_val, next_rows, conv_v)
    scale = float(POS * peers) ** (-0.5)
    (grad_w,) = call(lambda a, b: sum_body(a, b, scale=scale), [struct((2 * F, 2 * F), F32)], arrived)
    return (attended[None], grad_v[None], grad_w)


def solution(mesh):
    split = Mesh(
        mesh.devices.reshape(8, 4, 2, mesh.shape["fsdp"], mesh.shape["batch"]),
        ("ctx_0", "ctx_1", "ctx_2", "fsdp", "batch"),
    )
    in_specs = (
        P("batch", CTX, None),
        P("batch", CTX, "fsdp"),
        P("fsdp", None),
        P(None, "fsdp"),
        P(None, "fsdp"),
        P("batch", CTX, "fsdp"),
    )
    out_specs = (P("batch", CTX, "fsdp"), P("batch", CTX, "fsdp"), P(CTX_BATCH, "fsdp"))
    return jax.shard_map(
        shards, mesh=split, in_specs=in_specs, out_specs=out_specs, check_vma=False
    )
```
